32 devices in a mesh: dp: 16 (over z, y, x), tensor: 2 (over core).
Axes of the slice: x: 2, y: 2, z: 4, core: 2. Of those that a mesh axis runs over, the one named last changes fastest.
Arguments:
- features: bfloat16 [4096, 8192], P('dp', 'tensor'), may hold values from -6 to 6
- gate_pre: bfloat16 [4096, 14336], P('dp', 'tensor'), may hold values from -6 to 6
- up_pre: bfloat16 [4096, 14336], P('dp', 'tensor'), may hold values from -6 to 6
- grad_hidden: bfloat16 [4096, 14336], P('dp', 'tensor'), may hold values from -0.4375 to 0.4375
- blocks: int32 [32, 3], P('tensor'), may hold values from 0 to 63, as said below
- owner: int32 [32], P('tensor'), may hold values from 0 to 15, as said below
- weights: float32 [96, 128, 128], P(('dp', 'tensor')), may hold values from -0.4375 to 0.4375
- moment1: float32 [96, 128, 128], P(('dp', 'tensor')), may hold values from -6 to 6
- moment2: float32 [96, 128, 128], P(('dp', 'tensor')), may hold values from 0.05 to 2
Outputs:
- new_weights: float32 [96, 128, 128], P(('dp', 'tensor'))
- new_moment1: float32 [96, 128, 128], P(('dp', 'tensor'))
- new_moment2: float32 [96, 128, 128], P(('dp', 'tensor'))
The draws below stay inside these ranges and needn't reach their ends.
Inputs may be any that keep to these rules, and one draw needn't show every extreme that they name: Each row is (matrix, row block, column block): matrix 0 is the gate and 1 the up projection, row block below 64, column block below 56 and counted within the tensor index's own columns. The rows of one tensor index's list are distinct; columns hold unequal numbers of blocks. `owner`: in each tensor index's list no index of dp owns more than 3 blocks, and some index of dp owns exactly 3.
All inputs are finite; a program needn't handle non-finite values.
Results may differ from the reference program's by a relative error of at most 0.0028.
Values may be sent and summed in bfloat16 or wider, within the bound.
No kernel may reach another device: no remote copies, remote signals or barrier semaphores. Data moves between devices by JAX's collectives and lax.ppermute only.
A program may use at most 128 MiB of HBM per device.

```python
import math
import jax
import jax.numpy as jnp
from jax import lax

D = 8192
FF = 14336
BS = 128
CAP = 3
REPLICAS = 16
TENSORS = 2
TOKENS = 4096
NBT = 16
N_DP = 16
N_TENSOR = 2


def draw_blocks(key, part):
    row_count = D // BS
    col_count = FF // N_TENSOR // BS
    cell_count = 2 * row_count * col_count

    def one_list(subkey):
        first_key, second_key = jax.random.split(subkey)
        column_weight = jax.random.randint(first_key, (col_count,), 1, 9)
        base = jax.random.randint(second_key, (2, row_count, col_count), 0, 4096)
        score = (base * column_weight[None, None, :]).reshape(-1) * cell_count + jnp.arange(cell_count, dtype=jnp.int32)
        picked = lax.top_k(score, NBT)[1].astype(jnp.int32)
        matrix_id = picked // (row_count * col_count)
        row_id = picked // col_count % row_count
        col_id = picked % col_count
        return jnp.stack([matrix_id, row_id, col_id], axis=1)
    subkeys = jax.random.split(jax.random.fold_in(key, 11), N_TENSOR)
    return jax.vmap(one_list)(subkeys).reshape(N_TENSOR * NBT, 3).astype(jnp.int32)


def draw_owner(key, part):
    slot_total = N_DP * CAP

    def one_list(subkey):
        first_key, second_key, third_key = jax.random.split(subkey, 3)
        busiest = jax.random.randint(first_key, (), 0, N_DP)
        slots = jnp.arange(slot_total, dtype=jnp.int32)
        slot_owner = slots // CAP
        score = jax.random.randint(second_key, (slot_total,), 0, 1 << 20)
        ranking = jnp.where(slot_owner == busiest, slots, slot_total + score * slot_total + slots)
        picked = jnp.argsort(ranking, stable=True)[:NBT].astype(jnp.int32)
        owners = picked // CAP
        shuffle = jax.random.permutation(third_key, NBT)
        return owners[shuffle]
    subkeys = jax.random.split(jax.random.fold_in(key, 23), N_TENSOR)
    return jax.vmap(one_list)(subkeys).reshape(N_TENSOR * NBT).astype(jnp.int32)


def steps_of(stream_key, extent, cuts, low, top_value):
    gain, own = 1.0, jax.random.fold_in(stream_key, 6)
    for axis_at, parts in cuts:
        steps = jnp.exp(jax.random.uniform(jax.random.fold_in(own, axis_at), (parts,), jnp.float32, low / len(cuts), top_value / len(cuts)))
        gain = gain * jnp.repeat(steps, extent[axis_at] // parts).reshape([-1 if axis == axis_at else 1 for axis in range(len(extent))])
    return gain


def scatter_about(stream_key, extent, deviation, reach, cuts=(), kind=jnp.bfloat16):
    array = jax.random.normal(stream_key, extent, jnp.float32) * deviation
    if len(cuts) > 0:
        array = steps_of(stream_key, extent, cuts, -0.22, 0.18) * array
    return jnp.clip(array, min=-reach, max=reach).astype(kind)


def setup_inputs(seed: int = 0) -> dict:
    seeds = jax.random.split(jax.random.key(seed), 10)
    return {
        "features": scatter_about(seeds[0], (TOKENS, D), 1.0, 6.0, ((0, 16), (1, 2))),
        "gate_pre": scatter_about(seeds[1], (TOKENS, FF), 1.0, 6.0, ((0, 16), (1, 2))),
        "up_pre": scatter_about(seeds[2], (TOKENS, FF), 1.0, 6.0, ((0, 16), (1, 2))),
        "grad_hidden": scatter_about(seeds[3], (TOKENS, FF), 0.03, 0.4375, ((0, 16), (1, 2))),
        "blocks": draw_blocks(jax.random.fold_in(seeds[9], 71), 0),
        "owner": draw_owner(jax.random.fold_in(seeds[9], 71), 0),
        "weights": scatter_about(seeds[6], (REPLICAS * TENSORS * CAP, BS, BS), 0.03, 0.4375, ((0, 32),), jnp.float32),
        "moment1": scatter_about(seeds[7], (REPLICAS * TENSORS * CAP, BS, BS), 0.5, 6.0, ((0, 32),), jnp.float32),
        "moment2": jnp.clip(jnp.exp(math.log(2.0) - 3.6888794 * jax.random.uniform(seeds[8], (REPLICAS * TENSORS * CAP, BS, BS), jnp.float32) ** steps_of(seeds[8], (REPLICAS * TENSORS * CAP, BS, BS), ((0, 32),), -0.2, 0.2)), 0.05, 2.0),
    }


beta_first = 0.9
beta_second = 0.999
learn_rate = 0.01
epsilon = 1e-08
bias_first = 1.0 - 0.9 ** 10
bias_second = 1.0 - 0.999 ** 10

def slot_ranks(owners):
    count = owners.shape[0]
    earlier = lax.broadcasted_iota(jnp.int32, (count, count), 1) < lax.broadcasted_iota(jnp.int32, (count, count), 0)
    same_owner = owners[:, None] == owners[None, :]
    return lax.optimization_barrier(jnp.sum((same_owner & earlier).astype(jnp.int32), axis=1)).astype(jnp.int32)

def reference(features, gate_pre, up_pre, grad_hidden, blocks, owner, weights, moment1, moment2):
    columns = FF // N_TENSOR
    grads_list = []
    place_list = []
    for tensor_index in range(N_TENSOR):
        start_col = tensor_index * columns
        gate_value = gate_pre[:, start_col:start_col + columns].astype(jnp.float32)
        cotangent = grad_hidden[:, start_col:start_col + columns].astype(jnp.float32)
        up_value = up_pre[:, start_col:start_col + columns].astype(jnp.float32)
        sigmoid_gate = jax.nn.sigmoid(gate_value)
        grad_up = (cotangent * (gate_value * sigmoid_gate)).astype(jnp.bfloat16)
        grad_gate = (cotangent * up_value * (sigmoid_gate * (1.0 + gate_value * (1.0 - sigmoid_gate)))).astype(jnp.bfloat16)
        paired = jnp.concatenate([grad_gate, grad_up], axis=1)
        listing = blocks[tensor_index * NBT:(tensor_index + 1) * NBT]
        owners = owner[tensor_index * NBT:(tensor_index + 1) * NBT]

        def one_block(block_entry):
            rows_part = lax.dynamic_slice(features, (jnp.int32(0), block_entry[1] * BS), (TOKENS, BS))
            cols_part = lax.dynamic_slice(paired, (jnp.int32(0), block_entry[0] * columns + block_entry[2] * BS), (TOKENS, BS))
            return jnp.dot(rows_part.T, cols_part, preferred_element_type=jnp.float32)
        grads_list.append(lax.map(one_block, listing))
        place_list.append(((owners * N_TENSOR + tensor_index) * CAP + slot_ranks(owners)).astype(jnp.int32))
    block_grad = jnp.concatenate(grads_list, axis=0)
    places = jnp.concatenate(place_list, axis=0)
    first_old = moment1[places]
    second_old = moment2[places]
    weight_old = weights[places]
    first_new = beta_first * first_old + (1.0 - beta_first) * block_grad
    second_new = beta_second * second_old + (1.0 - beta_second) * block_grad * block_grad
    weight_new = weight_old - learn_rate * (first_new / bias_first) / (jnp.sqrt(second_new / bias_second) + epsilon)
    return (weights.at[places].set(weight_new), moment1.at[places].set(first_new), moment2.at[places].set(second_new))
```

```python
import functools
import jax
import jax.numpy as jnp
from jax import lax
from jax.experimental import pallas as pl
from jax.experimental.pallas import tpu as pltpu
from jax.sharding import PartitionSpec as P

beta_first = 0.9
beta_second = 0.999
learn_rate = 0.01
epsilon = 1e-08
bias_first = 1.0 - 0.9**10
bias_second = 1.0 - 0.999**10

ANY = pl.BlockSpec(memory_space=pl.ANY)
SMEM = pl.BlockSpec(memory_space=pltpu.SMEM)
VMEM = pl.BlockSpec(memory_space=pltpu.VMEM)


def act_kernel(blk, own, gate, up, cot, act, place, gbuf, ubuf, cbuf, sems, seen, *, capacity):
    listed, tokens, size = act.shape

    def copies(k):
        cols = pl.ds(pl.multiple_of(blk[2, k] * size, size), size)
        return [
            pltpu.make_async_copy(src.at[:, cols], buf.at[k], sems.at[i, k])
            for i, (src, buf) in enumerate(((gate, gbuf), (up, ubuf), (cot, cbuf)))
        ]

    def begin(k, carry):
        for copy in copies(k):
            copy.start()
        return carry

    lax.fori_loop(0, listed, begin, 0)

    def clear(o, carry):
        seen[o] = 0
        return carry

    lax.fori_loop(0, seen.shape[0], clear, 0)

    def rank(k, carry):
        o = own[k]
        slot = seen[o]
        seen[o] = slot + 1
        place[k] = o * capacity + slot
        return carry

    lax.fori_loop(0, listed, rank, 0)
    place[listed] = seen[lax.axis_index("dp")]

    def compute(k, carry):
        for copy in copies(k):
            copy.wait()
        g = gbuf[k].astype(jnp.float32)
        c = cbuf[k].astype(jnp.float32)
        s = jax.nn.sigmoid(g)

        @pl.when(blk[0, k] == 0)
        def _():
            u = ubuf[k].astype(jnp.float32)
            act[k] = (c * u * (s * (1.0 + g * (1.0 - s)))).astype(act.dtype)

        @pl.when(blk[0, k] != 0)
        def _():
            act[k] = (c * (g * s)).astype(act.dtype)

        return carry

    lax.fori_loop(0, listed, compute, 0)


def product_kernel(blk, place, act, *rest, shards):
    feats = rest[:shards]
    out, fbuf, sems = rest[shards:]
    listed, tokens, size = act.shape
    per = feats[0].shape[1] // size
    mine = lax.axis_index("tensor")

    def begin(k, carry):
        r = blk[1, k]
        source = lax.rem(mine + shards - r // per, shards)
        cols = pl.ds(pl.multiple_of(lax.rem(r, per) * size, size), size)
        for j in range(shards):

            @pl.when(source == j)
            def _():
                pltpu.make_async_copy(feats[j].at[:, cols], fbuf.at[k], sems.at[k]).start()

        return carry

    lax.fori_loop(0, listed, begin, 0)

    def compute(k, carry):
        pltpu.make_async_copy(feats[0].at[:, pl.ds(0, size)], fbuf.at[k], sems.at[k]).wait()
        out[place[k]] = lax.dot_general(
            fbuf[k], act[k], (((0,), (0,)), ((), ())), preferred_element_type=jnp.float32
        ).astype(out.dtype)
        return carry

    lax.fori_loop(0, listed, compute, 0)


def local(features, gate_pre, up_pre, grad_hidden, blocks, owner, weights, moment1, moment2):
    size = weights.shape[-1]
    capacity = weights.shape[0]
    replicas = lax.axis_size("dp")
    shards = lax.axis_size("tensor")
    listed = owner.shape[0]
    tokens = features.shape[0]
    bf16, f32 = jnp.bfloat16, jnp.float32
    table = blocks.T

    feats = [features] + [
        lax.ppermute(features, "tensor", [(i, (i + j) % shards) for i in range(shards)])
        for j in range(1, shards)
    ]
    act, place = pl.pallas_call(
        functools.partial(act_kernel, capacity=capacity),
        out_shape=(
            jax.ShapeDtypeStruct((listed, tokens, size), bf16),
            jax.ShapeDtypeStruct((listed + 1,), jnp.int32),
        ),
        in_specs=[SMEM, SMEM, ANY, ANY, ANY],
        out_specs=(VMEM, SMEM),
        scratch_shapes=[pltpu.VMEM((listed, tokens, size), bf16)] * 3
        + [pltpu.SemaphoreType.DMA((3, listed)), pltpu.SMEM((replicas,), jnp.int32)],
        name="activations",
    )(table, owner, gate_pre, up_pre, grad_hidden)
    outgoing = pl.pallas_call(
        functools.partial(product_kernel, shards=shards),
        out_shape=jax.ShapeDtypeStruct((replicas * capacity, size, size), bf16),
        in_specs=[SMEM, SMEM, VMEM] + [ANY] * shards,
        out_specs=VMEM,
        scratch_shapes=[
            pltpu.VMEM((listed, tokens, size), bf16),
            pltpu.SemaphoreType.DMA((listed,)),
        ],
        name="products",
    )(table, place, act, *feats)
    incoming = lax.all_to_all(outgoing, "dp", split_axis=0, concat_axis=0, tiled=True)
    block_grad = jnp.sum(
        incoming.astype(f32).reshape(replicas, capacity, size, size), axis=0
    )
    is_valid = (jnp.arange(capacity, dtype=jnp.int32) < place[listed])[:, None, None]
    first_new = beta_first * moment1 + (1.0 - beta_first) * block_grad
    second_new = beta_second * moment2 + (1.0 - beta_second) * block_grad * block_grad
    weight_new = weights - learn_rate * (first_new / bias_first) / (
        jnp.sqrt(second_new / bias_second) + epsilon
    )
    return (
        jnp.where(is_valid, weight_new, weights),
        jnp.where(is_valid, first_new, moment1),
        jnp.where(is_valid, second_new, moment2),
    )


def solution(mesh):
    cells = P(("dp", "tensor"), None, None)
    split = P("dp", "tensor")
    return jax.shard_map(
        local,
        mesh=mesh,
        in_specs=(split, split, split, split, P("tensor", None), P("tensor"), cells, cells, cells),
        out_specs=(cells, cells, cells),
        check_vma=False,
    )
```

```python
import functools
import jax
import jax.numpy as jnp
from jax import lax
from jax.experimental import pallas as pl
from jax.experimental.pallas import tpu as pltpu
from jax.sharding import PartitionSpec as P

beta_first = 0.9
beta_second = 0.999
learn_rate = 0.01
epsilon = 1e-08
bias_first = 1.0 - 0.9**10
bias_second = 1.0 - 0.999**10

HBM = pl.BlockSpec(memory_space=pltpu.HBM)
SMEM = pl.BlockSpec(memory_space=pltpu.SMEM)
VMEM = pl.BlockSpec(memory_space=pltpu.VMEM)

COLUMNS = 4


def bin_slots(listed, replicas, capacity):
    crowd = min(listed, capacity * replicas // COLUMNS)
    return max(-(-listed // 3), -(-crowd // 2))


def route(own, place, seen, work, *, capacity, slots):
    listed = own.shape[0]
    replicas = seen.shape[0]
    me = lax.axis_index("dp")
    column = lax.rem(me, COLUMNS)
    my_bit = (lax.rem(column, 2), column // 2)
    COUNT, RANK, TAKE, AT_A, AT_B, LOAD = (i * COLUMNS for i in range(6))

    def clear_seen(o, carry):
        seen[o] = 0
        return carry

    lax.fori_loop(0, replicas, clear_seen, 0)
    for i in range(6 * COLUMNS):
        work[i] = 0

    def count(k, carry):
        q = lax.rem(own[k], COLUMNS)
        work[COUNT + q] = work[COUNT + q] + 1
        return carry

    lax.fori_loop(0, listed, count, 0)

    first, most = jnp.int32(0), work[COUNT]
    for q in range(1, COLUMNS):
        n = work[COUNT + q]
        first = jnp.where(n > most, q, first)
        most = jnp.maximum(n, most)
    for i in range(COLUMNS):
        q = jnp.bitwise_xor(first, i)
        bin_a = LOAD + lax.rem(q, 2)
        bin_b = LOAD + 2 + q // 2
        n, load_a, load_b = work[COUNT + q], work[bin_a], work[bin_b]
        take = jnp.clip(lax.shift_right_arithmetic(n + load_b - load_a, 1), 0, n)
        work[TAKE + q] = take
        work[AT_A + q] = load_a
        work[AT_B + q] = load_b
        work[bin_a] = load_a + take
        work[bin_b] = load_b + n - take

    def clear_place(j, carry):
        place[listed + j] = 0
        return carry

    lax.fori_loop(0, replicas // COLUMNS * capacity, clear_place, 0)

    def assign(k, carry):
        o = own[k]
        q = lax.rem(o, COLUMNS)
        r = work[RANK + q]
        work[RANK + q] = r + 1
        take = work[TAKE + q]
        in_a = r < take
        slot = jnp.where(in_a, work[AT_A + q] + r, work[AT_B + q] + r - take)
        bit = jnp.where(in_a, lax.rem(q, 2), q // 2)
        mine = jnp.where(in_a, my_bit[0], my_bit[1])
        keep = (bit == mine).astype(jnp.int32)
        place[k] = jnp.where(in_a, 0, 2 * slots) + keep * slots + slot
        s = seen[o]
        seen[o] = s + 1

        @pl.when(q == column)
        def _():
            place[listed + o // COLUMNS * capacity + s] = jnp.where(in_a, 0, slots) + slot

        return carry

    lax.fori_loop(0, listed, assign, 0)
    place[place.shape[0] - 1] = seen[me]


def act_kernel(blk, own, features, gate, up, cot, *rest, capacity, slots):
    states, rest = rest[:3], rest[3:]
    act, rows, place = rest[:3]
    held, (gbuf, ubuf, cbuf, sems, state_sems, seen, work) = rest[3:6], rest[6:]
    listed, tokens, size = act.shape
    per = features.shape[1] // size

    def row_copy(k):
        cols = pl.ds(pl.multiple_of(lax.rem(blk[1, k], per) * size, size), size)
        return pltpu.make_async_copy(features.at[:, cols], rows.at[k], sems.at[3, k])

    def copies(k):
        cols = pl.ds(pl.multiple_of(blk[2, k] * size, size), size)
        return [
            pltpu.make_async_copy(src.at[:, cols], buf.at[k], sems.at[i, k])
            for i, (src, buf) in enumerate(((gate, gbuf), (up, ubuf), (cot, cbuf)))
        ]

    def begin(k, carry):
        for copy in copies(k):
            copy.start()
        return carry

    def begin_rows(k, carry):
        row_copy(k).start()
        return carry

    lax.fori_loop(0, listed, begin, 0)
    lax.fori_loop(0, listed, begin_rows, 0)
    state_copies = [
        pltpu.make_async_copy(src, dst, state_sems.at[i])
        for i, (src, dst) in enumerate(zip(states, held))
    ]
    for copy in state_copies:
        copy.start()
    route(own, place, seen, work, capacity=capacity, slots=slots)

    def compute(k, carry):
        for copy in copies(k):
            copy.wait()
        gated = blk[0, k] == 0
        g = gbuf[k].astype(jnp.float32)
        c = cbuf[k].astype(jnp.float32)
        s = jax.nn.sigmoid(g)
        first = jnp.where(gated, c * ubuf[k].astype(jnp.float32), c)
        act[k] = (first * jnp.where(gated, s * (1.0 + g * (1.0 - s)), g * s)).astype(act.dtype)
        return carry

    lax.fori_loop(0, listed, compute, 0)

    def end_rows(k, carry):
        row_copy(k).wait()
        return carry

    lax.fori_loop(0, listed, end_rows, 0)
    for copy in state_copies:
        copy.wait()


def product_kernel(blk, place, act, rows, *rest, shards, slots):
    others = rest[: shards - 1]
    send_a, send_b, part = rest[shards - 1 :]
    listed, tokens, size = act.shape
    per = others[0].shape[1] // size
    mine = lax.axis_index("tensor")

    def compute(k, carry):
        r = blk[1, k]
        cols = pl.ds(pl.multiple_of(lax.rem(r, per) * size, size), size)
        source = lax.rem(mine + shards - r // per, shards)
        lhs = rows[k]
        for j in range(1, shards):
            lhs = jnp.where(source == j, others[j - 1][:, cols], lhs)
        part[place[k]] = lax.dot_general(
            lhs, act[k], (((0,), (0,)), ((), ())), preferred_element_type=jnp.float32
        )
        return carry

    lax.fori_loop(0, listed, compute, 0, unroll=4)
    send_a[...] = part[:slots].astype(send_a.dtype)
    send_b[...] = part[2 * slots : 3 * slots].astype(send_b.dtype)


def add_kernel(part, got, total, send, *, start):
    total[...] = part[start : start + total.shape[0]] + got[...].astype(total.dtype)
    send[...] = total[...].astype(send.dtype)


def plane_kernel(place, sum_a, sum_b, other_a, other_b, *outs, listed, capacity):
    kept, sends = outs[0], outs[1:]
    slots = sum_a.shape[0]
    plane = lax.axis_index("dp") // COLUMNS

    def total(z, s):
        j = place[listed + z * capacity + s]
        a = jnp.minimum(j, slots - 1)
        b = jnp.maximum(j - slots, 0)
        return jnp.where(
            j < slots,
            sum_a[a] + other_a[a].astype(jnp.float32),
            sum_b[b] + other_b[b].astype(jnp.float32),
        )

    if len(sends) == 1:
        sends = sends[0]

        def lay(j, carry):
            sends[j] = total(j // capacity, lax.rem(j, capacity)).astype(sends.dtype)
            return carry

        lax.fori_loop(0, sends.shape[0], lay, 0)
    else:
        for k, send in enumerate(sends):
            for s in range(capacity):
                send[s] = total(jnp.bitwise_xor(plane, k + 1), s).astype(send.dtype)
    for s in range(capacity):
        kept[s] = total(plane, s)


def update_kernel(place, kept, *rest, count):
    parts, rest = rest[:count], rest[count:]
    weights, moment1, moment2, *outs = rest
    outs, (bufs, sems) = outs[:3], outs[3:]
    held = place[place.shape[0] - 1]
    copies = []
    for s in range(kept.shape[0]):
        valid = s < held
        block_grad = kept[s]
        for part in parts:
            block_grad = block_grad + part[s].astype(jnp.float32)
        first_new = beta_first * moment1[s] + (1.0 - beta_first) * block_grad
        second_new = beta_second * moment2[s] + (1.0 - beta_second) * block_grad * block_grad
        weight_new = weights[s] - learn_rate * (first_new / bias_first) / (
            jnp.sqrt(second_new / bias_second) + epsilon
        )
        bufs[0, s] = jnp.where(valid, weight_new, weights[s])
        bufs[1, s] = jnp.where(valid, first_new, moment1[s])
        bufs[2, s] = jnp.where(valid, second_new, moment2[s])
        for i, out in enumerate(outs):
            copy = pltpu.make_async_copy(bufs.at[i, s], out.at[s], sems.at[i, s])
            copy.start()
            copies.append(copy)
    for copy in copies:
        copy.wait()


def local(features, gate_pre, up_pre, grad_hidden, blocks, owner, weights, moment1, moment2):
    size = weights.shape[-1]
    capacity = weights.shape[0]
    replicas = lax.axis_size("dp")
    shards = lax.axis_size("tensor")
    listed = owner.shape[0]
    tokens = features.shape[0]
    planes = replicas // COLUMNS
    slots = bin_slots(listed, replicas, capacity)
    bf16, f32 = jnp.bfloat16, jnp.float32
    table = blocks.T
    block = size * size
    column = tokens * size
    in_vmem = lambda n, dtype: pltpu.VMEM((n, size, size), dtype)
    swap = lambda v, bit: lax.ppermute(v, "dp", [(i, i ^ bit) for i in range(replicas)])
    stay = lambda v: pltpu.with_memory_space_constraint(v, pltpu.HBM)
    grant = lambda nbytes: pltpu.CompilerParams(vmem_limit_bytes=nbytes * 5 // 4 + (4 << 20))

    others = [
        lax.ppermute(features, "tensor", [(i, (i + j) % shards) for i in range(shards)])
        for j in range(1, shards)
    ]
    act, rows, place, *states = pl.pallas_call(
        functools.partial(act_kernel, capacity=capacity, slots=slots),
        out_shape=(
            pltpu.VMEM((listed, tokens, size), bf16),
            pltpu.VMEM((listed, tokens, size), bf16),
            jax.ShapeDtypeStruct((listed + planes * capacity + 1,), jnp.int32),
        )
        + (in_vmem(capacity, f32),) * 3,
        in_specs=[SMEM, SMEM] + [HBM] * 7,
        out_specs=(VMEM, VMEM, SMEM, VMEM, VMEM, VMEM),
        scratch_shapes=[pltpu.VMEM((listed, tokens, size), bf16)] * 3
        + [
            pltpu.SemaphoreType.DMA((4, listed)),
            pltpu.SemaphoreType.DMA((3,)),
            pltpu.SMEM((replicas,), jnp.int32),
            pltpu.SMEM((6 * COLUMNS,), jnp.int32),
        ],
        compiler_params=grant(5 * listed * column * 2 + 3 * capacity * block * 4),
        name="activations",
    )(table, owner, *map(stay, (features, gate_pre, up_pre, grad_hidden, weights, moment1, moment2)))
    send_a, send_b, part = pl.pallas_call(
        functools.partial(product_kernel, shards=shards, slots=slots),
        out_shape=(in_vmem(slots, bf16), in_vmem(slots, bf16), in_vmem(4 * slots, f32)),
        in_specs=[SMEM, SMEM] + [VMEM] * (shards + 1),
        out_specs=(VMEM, VMEM, VMEM),
        compiler_params=grant(
            2 * listed * column * 2 + (shards - 1) * features.size * 2 + 20 * slots * block
        ),
        name="products",
    )(table, place, act, rows, *others)

    def add(got, start):
        return pl.pallas_call(
            functools.partial(add_kernel, start=start),
            out_shape=(in_vmem(slots, f32), in_vmem(slots, bf16)),
            in_specs=[VMEM, VMEM],
            out_specs=(VMEM, VMEM),
            compiler_params=grant(24 * slots * block),
            name="sums",
        )(part, got)

    sum_a, send_a = add(swap(send_a, 1), slots)
    sum_b, send_b = add(swap(send_b, 2), 3 * slots)
    other_a = swap(send_a, 2)
    other_b = swap(send_b, 1)
    direct = planes <= 4 and planes & (planes - 1) == 0
    kept, *sends = pl.pallas_call(
        functools.partial(plane_kernel, listed=listed, capacity=capacity),
        out_shape=(in_vmem(capacity, f32),)
        + ((in_vmem(capacity, bf16),) * (planes - 1) if direct else (in_vmem(planes * capacity, bf16),)),
        in_specs=[SMEM, VMEM, VMEM, VMEM, VMEM],
        out_specs=(VMEM,) * (planes if direct else 2),
        compiler_params=grant((12 * slots + (4 + 2 * planes) * capacity) * block),
        name="planes",
    )(place, sum_a, sum_b, other_a, other_b)
    if direct:
        parts = [swap(send, (k + 1) * COLUMNS) for k, send in enumerate(sends)]
    else:
        groups = [[z * COLUMNS + c for z in range(planes)] for c in range(COLUMNS)]
        incoming = lax.all_to_all(
            sends[0], "dp", split_axis=0, concat_axis=0, tiled=True, axis_index_groups=groups
        )
        away = jnp.arange(planes) != lax.axis_index("dp") // COLUMNS
        incoming = incoming.astype(f32).reshape(planes, capacity, size, size)
        parts = [jnp.sum(jnp.where(away[:, None, None, None], incoming, 0.0), axis=0)]
    return pl.pallas_call(
        functools.partial(update_kernel, count=len(parts)),
        out_shape=(jax.ShapeDtypeStruct(weights.shape, f32),) * 3,
        in_specs=[SMEM] + [VMEM] * (4 + len(parts)),
        out_specs=(HBM, HBM, HBM),
        scratch_shapes=[
            pltpu.VMEM((3,) + weights.shape, f32),
            pltpu.SemaphoreType.DMA((3, capacity)),
        ],
        compiler_params=grant((28 + 4 * len(parts)) * capacity * block),
        name="update",
    )(place, kept, *parts, *states)


def solution(mesh):
    cells = P(("dp", "tensor"), None, None)
    split = P("dp", "tensor")
    return jax.shard_map(
        local,
        mesh=mesh,
        in_specs=(split, split, split, split, P("tensor", None), P("tensor"), cells, cells, cells),
        out_specs=(cells, cells, cells),
        check_vma=False,
    )
```

```python
import functools
import jax
import jax.numpy as jnp
from jax import lax
from jax.experimental import pallas as pl
from jax.experimental.pallas import tpu as pltpu
from jax.sharding import PartitionSpec as P

beta_first = 0.9
beta_second = 0.999
learn_rate = 0.01
epsilon = 1e-08
bias_first = 1.0 - 0.9**10
bias_second = 1.0 - 0.999**10

HBM = pl.BlockSpec(memory_space=pltpu.HBM)
SMEM = pl.BlockSpec(memory_space=pltpu.SMEM)
VMEM = pl.BlockSpec(memory_space=pltpu.VMEM)

COLUMNS = 4


def bin_slots(listed, replicas, capacity):
    crowd = min(listed, capacity * replicas // COLUMNS)
    return max(-(-listed // 3), -(-crowd // 2))


def route(blk, own, place, seen, work, *, capacity, slots):
    listed = own.shape[0]
    replicas = seen.shape[0]
    me = lax.axis_index("dp")
    column = lax.rem(me, COLUMNS)
    my_bit = (lax.rem(column, 2), column // 2)
    COUNT, RANK, TAKE, AT_A, AT_B, LOAD = (i * COLUMNS for i in range(6))

    def clear_seen(o, carry):
        seen[o] = 0
        return carry

    lax.fori_loop(0, replicas, clear_seen, 0)
    for i in range(6 * COLUMNS):
        work[i] = 0

    def count(k, carry):
        q = lax.rem(own[k], COLUMNS)
        work[COUNT + q] = work[COUNT + q] + 1
        return carry

    lax.fori_loop(0, listed, count, 0)

    first, most = jnp.int32(0), work[COUNT]
    for q in range(1, COLUMNS):
        n = work[COUNT + q]
        first = jnp.where(n > most, q, first)
        most = jnp.maximum(n, most)
    for i in range(COLUMNS):
        q = jnp.bitwise_xor(first, i)
        bin_a = LOAD + lax.rem(q, 2)
        bin_b = LOAD + 2 + q // 2
        n, load_a, load_b = work[COUNT + q], work[bin_a], work[bin_b]
        take = jnp.clip(lax.shift_right_arithmetic(n + load_b - load_a, 1), 0, n)
        work[TAKE + q] = take
        work[AT_A + q] = load_a
        work[AT_B + q] = load_b
        work[bin_a] = load_a + take
        work[bin_b] = load_b + n - take

    def clear_place(j, carry):
        place[2 * listed + j] = 0
        return carry

    lax.fori_loop(0, replicas // COLUMNS * capacity, clear_place, 0)

    def assign(k, carry):
        o = own[k]
        q = lax.rem(o, COLUMNS)
        r = work[RANK + q]
        work[RANK + q] = r + 1
        take = work[TAKE + q]
        in_a = r < take
        slot = jnp.where(in_a, work[AT_A + q] + r, work[AT_B + q] + r - take)
        bit = jnp.where(in_a, lax.rem(q, 2), q // 2)
        mine = jnp.where(in_a, my_bit[0], my_bit[1])
        keep = (bit == mine).astype(jnp.int32)
        place[k] = jnp.where(in_a, 0, 2 * slots) + keep * slots + slot
        place[listed + k] = blk[1, k]
        s = seen[o]
        seen[o] = s + 1

        @pl.when(q == column)
        def _():
            place[2 * listed + o // COLUMNS * capacity + s] = jnp.where(in_a, 0, slots) + slot

        return carry

    lax.fori_loop(0, listed, assign, 0)
    place[place.shape[0] - 1] = seen[me]


def act_kernel(blk_hbm, own_hbm, features, gate, up, cot, *rest, capacity, slots):
    states, rest = rest[:3], rest[3:]
    act, rows, place = rest[:3]
    held, (gbuf, ubuf, cbuf, blk, own, sems, state_sems, seen, work) = rest[3:6], rest[6:]
    listed, tokens, size = act.shape
    per = features.shape[1] // size
    mine = lax.axis_index("tensor")

    def row_copy(k):
        cols = pl.ds(pl.multiple_of(lax.rem(blk[1, k], per) * size, size), size)
        return pltpu.make_async_copy(features.at[:, cols], rows.at[k], sems.at[3, k])

    def copies(k):
        cols = pl.ds(pl.multiple_of(blk[2, k] * size, size), size)
        return [
            pltpu.make_async_copy(src.at[:, cols], buf.at[k], sems.at[i, k])
            for i, (src, buf) in enumerate(((gate, gbuf), (up, ubuf), (cot, cbuf)))
        ]

    def begin(k, carry):
        gated = blk[0, k] == 0
        first, second, third = copies(k)
        first.start()
        third.start()
        pl.when(gated)(second.start)
        return carry

    def begin_rows(k, carry):
        pl.when(blk[1, k] // per == mine)(row_copy(k).start)
        return carry

    tables = [
        pltpu.make_async_copy(blk_hbm, blk, state_sems.at[3]),
        pltpu.make_async_copy(own_hbm, own, state_sems.at[4]),
    ]
    for copy in tables:
        copy.start()
    tables[0].wait()
    lax.fori_loop(0, listed, begin, 0, unroll=2)
    lax.fori_loop(0, listed, begin_rows, 0, unroll=2)
    state_copies = [
        pltpu.make_async_copy(src, dst, state_sems.at[i])
        for i, (src, dst) in enumerate(zip(states, held))
    ]
    for copy in state_copies:
        copy.start()
    tables[1].wait()
    route(blk, own, place, seen, work, capacity=capacity, slots=slots)

    def compute(k, carry):
        gated = blk[0, k] == 0
        first, second, third = copies(k)
        first.wait()
        third.wait()
        pl.when(gated)(second.wait)
        g = gbuf[k].astype(jnp.float32)
        c = cbuf[k].astype(jnp.float32)
        s = jax.nn.sigmoid(g)
        first = jnp.where(gated, c * ubuf[k].astype(jnp.float32), c)
        act[k] = (first * jnp.where(gated, s * (1.0 + g * (1.0 - s)), g * s)).astype(act.dtype)
        return carry

    lax.fori_loop(0, listed, compute, 0, unroll=2)

    def end_rows(k, carry):
        pl.when(blk[1, k] // per == mine)(row_copy(k).wait)
        return carry

    lax.fori_loop(0, listed, end_rows, 0)
    for copy in state_copies:
        copy.wait()


def product_kernel(place, act, rows, *rest, shards, slots):
    others = rest[: shards - 1]
    send_a, send_b, part = rest[shards - 1 :]
    listed, tokens, size = act.shape
    per = others[0].shape[1] // size
    mine = lax.axis_index("tensor")

    def compute(k, carry):
        r = place[listed + k]
        cols = pl.ds(pl.multiple_of(lax.rem(r, per) * size, size), size)
        source = lax.rem(mine + shards - r // per, shards)
        lhs = rows[k]
        for j in range(1, shards):
            lhs = jnp.where(source == j, others[j - 1][:, cols], lhs)
        part[place[k]] = lax.dot_general(
            lhs, act[k], (((0,), (0,)), ((), ())), preferred_element_type=jnp.float32
        )
        return carry

    lax.fori_loop(0, listed, compute, 0, unroll=16)
    send_a[...] = part[:slots].astype(send_a.dtype)
    send_b[...] = part[2 * slots : 3 * slots].astype(send_b.dtype)


def add_kernel(part, got, total, send, *, start):
    total[...] = part[start : start + total.shape[0]] + got[...].astype(total.dtype)
    send[...] = total[...].astype(send.dtype)


def plane_kernel(place, sum_a, sum_b, other_a, other_b, *outs, listed, capacity):
    kept, sends = outs[0], outs[1:]
    slots = sum_a.shape[0]
    plane = lax.axis_index("dp") // COLUMNS

    def total(z, s):
        j = place[2 * listed + z * capacity + s]
        a = jnp.minimum(j, slots - 1)
        b = jnp.maximum(j - slots, 0)
        return jnp.where(
            j < slots,
            sum_a[a] + other_a[a].astype(jnp.float32),
            sum_b[b] + other_b[b].astype(jnp.float32),
        )

    if len(sends) == 1:
        sends = sends[0]

        def lay(j, carry):
            sends[j] = total(j // capacity, lax.rem(j, capacity)).astype(sends.dtype)
            return carry

        lax.fori_loop(0, sends.shape[0], lay, 0)
    else:
        for k, send in enumerate(sends):
            for s in range(capacity):
                send[s] = total(jnp.bitwise_xor(plane, k + 1), s).astype(send.dtype)
    for s in range(capacity):
        kept[s] = total(plane, s)


def update_kernel(place, kept, *rest, count):
    parts, rest = rest[:count], rest[count:]
    weights, moment1, moment2, *outs = rest
    outs, (bufs, sems) = outs[:3], outs[3:]
    held = place[place.shape[0] - 1]
    copies = []
    for s in range(kept.shape[0]):
        valid = s < held
        block_grad = kept[s]
        for part in parts:
            block_grad = block_grad + part[s].astype(jnp.float32)
        first_new = beta_first * moment1[s] + (1.0 - beta_first) * block_grad
        second_new = beta_second * moment2[s] + (1.0 - beta_second) * block_grad * block_grad
        weight_new = weights[s] - learn_rate * (first_new / bias_first) / (
            jnp.sqrt(second_new / bias_second) + epsilon
        )
        bufs[0, s] = jnp.where(valid, weight_new, weights[s])
        bufs[1, s] = jnp.where(valid, first_new, moment1[s])
        bufs[2, s] = jnp.where(valid, second_new, moment2[s])
        for i, out in enumerate(outs):
            copy = pltpu.make_async_copy(bufs.at[i, s], out.at[s], sems.at[i, s])
            copy.start()
            copies.append(copy)
    for copy in copies:
        copy.wait()


def local(features, gate_pre, up_pre, grad_hidden, blocks, owner, weights, moment1, moment2):
    size = weights.shape[-1]
    capacity = weights.shape[0]
    replicas = lax.axis_size("dp")
    shards = lax.axis_size("tensor")
    listed = owner.shape[0]
    tokens = features.shape[0]
    planes = replicas // COLUMNS
    slots = bin_slots(listed, replicas, capacity)
    bf16, f32 = jnp.bfloat16, jnp.float32
    block = size * size
    column = tokens * size
    in_vmem = lambda n, dtype: pltpu.VMEM((n, size, size), dtype)
    swap = lambda v, bit: lax.ppermute(v, "dp", [(i, i ^ bit) for i in range(replicas)])
    stay = lambda v: pltpu.with_memory_space_constraint(v, pltpu.HBM)
    grant = lambda nbytes: pltpu.CompilerParams(vmem_limit_bytes=nbytes * 5 // 4 + (4 << 20))

    others = [
        lax.ppermute(features, "tensor", [(i, (i + j) % shards) for i in range(shards)])
        for j in range(1, shards)
    ]
    act, rows, place, *states = pl.pallas_call(
        functools.partial(act_kernel, capacity=capacity, slots=slots),
        out_shape=(
            pltpu.VMEM((listed, tokens, size), bf16),
            pltpu.VMEM((listed, tokens, size), bf16),
            pltpu.SMEM((2 * listed + planes * capacity + 1,), jnp.int32),
        )
        + (in_vmem(capacity, f32),) * 3,
        in_specs=[HBM] * 9,
        out_specs=(VMEM, VMEM, SMEM, VMEM, VMEM, VMEM),
        scratch_shapes=[pltpu.VMEM((listed, tokens, size), bf16)] * 3
        + [
            pltpu.SMEM((3, listed), jnp.int32),
            pltpu.SMEM((listed,), jnp.int32),
            pltpu.SemaphoreType.DMA((4, listed)),
            pltpu.SemaphoreType.DMA((5,)),
            pltpu.SMEM((replicas,), jnp.int32),
            pltpu.SMEM((6 * COLUMNS,), jnp.int32),
        ],
        compiler_params=grant(5 * listed * column * 2 + 3 * capacity * block * 4),
        name="activations",
    )(*map(stay, (blocks.T, owner, features, gate_pre, up_pre, grad_hidden, weights, moment1, moment2)))
    send_a, send_b, part = pl.pallas_call(
        functools.partial(product_kernel, shards=shards, slots=slots),
        out_shape=(in_vmem(slots, bf16), in_vmem(slots, bf16), in_vmem(4 * slots, f32)),
        in_specs=[SMEM] + [VMEM] * (shards + 1),
        out_specs=(VMEM, VMEM, VMEM),
        compiler_params=grant(
            2 * listed * column * 2 + (shards - 1) * features.size * 2 + 20 * slots * block
        ),
        name="products",
    )(place, act, rows, *others)

    def add(got, start):
        return pl.pallas_call(
            functools.partial(add_kernel, start=start),
            out_shape=(in_vmem(slots, f32), in_vmem(slots, bf16)),
            in_specs=[VMEM, VMEM],
            out_specs=(VMEM, VMEM),
            compiler_params=grant(24 * slots * block),
            name="sums",
        )(part, got)

    sum_a, send_a = add(swap(send_a, 1), slots)
    sum_b, send_b = add(swap(send_b, 2), 3 * slots)
    other_a = swap(send_a, 2)
    other_b = swap(send_b, 1)
    direct = planes <= 4 and planes & (planes - 1) == 0
    kept, *sends = pl.pallas_call(
        functools.partial(plane_kernel, listed=listed, capacity=capacity),
        out_shape=(in_vmem(capacity, f32),)
        + ((in_vmem(capacity, bf16),) * (planes - 1) if direct else (in_vmem(planes * capacity, bf16),)),
        in_specs=[SMEM, VMEM, VMEM, VMEM, VMEM],
        out_specs=(VMEM,) * (planes if direct else 2),
        compiler_params=grant((12 * slots + (4 + 2 * planes) * capacity) * block),
        name="planes",
    )(place, sum_a, sum_b, other_a, other_b)
    if direct:
        parts = [swap(send, (k + 1) * COLUMNS) for k, send in enumerate(sends)]
    else:
        groups = [[z * COLUMNS + c for z in range(planes)] for c in range(COLUMNS)]
        incoming = lax.all_to_all(
            sends[0], "dp", split_axis=0, concat_axis=0, tiled=True, axis_index_groups=groups
        )
        away = jnp.arange(planes) != lax.axis_index("dp") // COLUMNS
        incoming = incoming.astype(f32).reshape(planes, capacity, size, size)
        parts = [jnp.sum(jnp.where(away[:, None, None, None], incoming, 0.0), axis=0)]
    return pl.pallas_call(
        functools.partial(update_kernel, count=len(parts)),
        out_shape=(jax.ShapeDtypeStruct(weights.shape, f32),) * 3,
        in_specs=[SMEM] + [VMEM] * (4 + len(parts)),
        out_specs=(HBM, HBM, HBM),
        scratch_shapes=[
            pltpu.VMEM((3,) + weights.shape, f32),
            pltpu.SemaphoreType.DMA((3, capacity)),
        ],
        compiler_params=grant((28 + 4 * len(parts)) * capacity * block),
        name="update",
    )(place, kept, *parts, *states)


def solution(mesh):
    cells = P(("dp", "tensor"), None, None)
    split = P("dp", "tensor")
    return jax.shard_map(
        local,
        mesh=mesh,
        in_specs=(split, split, split, split, P("tensor", None), P("tensor"), cells, cells, cells),
        out_specs=(cells, cells, cells),
        check_vma=False,
    )
```

```python
import functools
import jax
import jax.numpy as jnp
from jax import lax
from jax.experimental import pallas as pl
from jax.experimental.pallas import tpu as pltpu
from jax.sharding import PartitionSpec as P

beta_first = 0.9
beta_second = 0.999
learn_rate = 0.01
epsilon = 1e-08
bias_first = 1.0 - 0.9**10
bias_second = 1.0 - 0.999**10

HBM = pl.BlockSpec(memory_space=pltpu.HBM)
SMEM = pl.BlockSpec(memory_space=pltpu.SMEM)
VMEM = pl.BlockSpec(memory_space=pltpu.VMEM)

COLUMNS = 4


def bin_sizes(listed, replicas, capacity):
    crowd = min(listed, capacity * replicas // COLUMNS)
    level, most = -(-listed // COLUMNS), max(-(-listed // 3), -(-crowd // 2))
    return sorted({min(level, most), min(level + max(listed // 16, 1), most), most})


def route(blk, own, place, flag, seen, work, *, capacity, sizes):
    listed = own.shape[0]
    replicas = seen.shape[0]
    me = lax.axis_index("dp")
    column = lax.rem(me, COLUMNS)
    my_bit = (lax.rem(column, 2), column // 2)
    COUNT, RANK, TAKE, AT_A, AT_B, LOAD = (i * COLUMNS for i in range(6))

    def clear_seen(o, carry):
        seen[o] = 0
        return carry

    lax.fori_loop(0, replicas, clear_seen, 0)
    for i in range(6 * COLUMNS):
        work[i] = 0

    def count(k, carry):
        q = lax.rem(own[k], COLUMNS)
        work[COUNT + q] = work[COUNT + q] + 1
        return carry

    lax.fori_loop(0, listed, count, 0)

    n = [work[COUNT + q] for q in range(COLUMNS)]

    def shares(size, a0):
        a2 = jnp.minimum(n[2], size - a0)
        a1 = n[1] - jnp.minimum(n[1], size - (n[0] - a0))
        a3 = jnp.minimum(n[3], size - a1)
        return a0, a1, a2, a3

    def search(size):
        low = jnp.maximum(n[0] - size, 0)
        high = jnp.minimum(n[0], size)

        def attempt(i, best):
            a = shares(size, low + i)
            ok = (low + i <= high) & (a[1] <= size) & (n[2] - a[2] + n[3] - a[3] <= size)
            return jnp.where(ok, low + i, best)

        return lax.fori_loop(0, size + 1, attempt, jnp.int32(-1))

    flag[0] = len(sizes) - 1
    work[LOAD + 1] = sizes[-1]
    work[LOAD] = search(sizes[-1])
    for i in reversed(range(len(sizes) - 1)):
        best = search(sizes[i])

        @pl.when(best >= 0)
        def _():
            flag[0] = i
            work[LOAD + 1] = sizes[i]
            work[LOAD] = best

    slots = work[LOAD + 1]
    a = shares(slots, work[LOAD])
    for q in range(COLUMNS):
        work[TAKE + q] = a[q]
    for q, (at_a, at_b) in enumerate(((0, 0), (0, n[0] - a[0]), (a[0], 0), (a[1], n[2] - a[2]))):
        work[AT_A + q] = at_a
        work[AT_B + q] = at_b

    def clear_place(j, carry):
        place[2 * listed + j] = 0
        return carry

    lax.fori_loop(0, replicas // COLUMNS * capacity, clear_place, 0)

    def assign(k, carry):
        o = own[k]
        q = lax.rem(o, COLUMNS)
        r = work[RANK + q]
        work[RANK + q] = r + 1
        take = work[TAKE + q]
        in_a = r < take
        slot = jnp.where(in_a, work[AT_A + q] + r, work[AT_B + q] + r - take)
        bit = jnp.where(in_a, lax.rem(q, 2), q // 2)
        mine = jnp.where(in_a, my_bit[0], my_bit[1])
        keep = (bit == mine).astype(jnp.int32)
        place[k] = jnp.where(in_a, 0, 2 * slots) + keep * slots + slot
        place[listed + k] = blk[1, k]
        s = seen[o]
        seen[o] = s + 1

        @pl.when(q == column)
        def _():
            place[2 * listed + o // COLUMNS * capacity + s] = jnp.where(in_a, 0, slots) + slot

        return carry

    lax.fori_loop(0, listed, assign, 0)
    place[place.shape[0] - 1] = seen[me]


def act_kernel(blk_hbm, own_hbm, features, gate, up, cot, *rest, capacity, sizes):
    states, rest = rest[:3], rest[3:]
    act, rows, place, flag = rest[:4]
    held, (gbuf, ubuf, cbuf, blk, own, sems, state_sems, seen, work) = rest[4:7], rest[7:]
    listed, _, size = act.shape
    per = features.shape[1] // size
    mine = lax.axis_index("tensor")

    def row_copy(k):
        cols = pl.ds(pl.multiple_of(lax.rem(blk[1, k], per) * size, size), size)
        return pltpu.make_async_copy(features.at[:, cols], rows.at[k], sems.at[3, k])

    def copies(k):
        cols = pl.ds(pl.multiple_of(blk[2, k] * size, size), size)
        return [
            pltpu.make_async_copy(src.at[:, cols], buf.at[k], sems.at[i, k])
            for i, (src, buf) in enumerate(((gate, gbuf), (up, ubuf), (cot, cbuf)))
        ]

    def begin(k, carry):
        gated = blk[0, k] == 0
        first, second, third = copies(k)
        first.start()
        third.start()
        pl.when(gated)(second.start)
        return carry

    def begin_rows(k, carry):
        pl.when(blk[1, k] // per == mine)(row_copy(k).start)
        return carry

    tables = [
        pltpu.make_async_copy(blk_hbm, blk, state_sems.at[3]),
        pltpu.make_async_copy(own_hbm, own, state_sems.at[4]),
    ]
    for copy in tables:
        copy.start()
    tables[0].wait()
    lax.fori_loop(0, listed, begin, 0, unroll=2)
    lax.fori_loop(0, listed, begin_rows, 0, unroll=2)
    state_copies = [
        pltpu.make_async_copy(src, dst, state_sems.at[i])
        for i, (src, dst) in enumerate(zip(states, held))
    ]
    for copy in state_copies:
        copy.start()
    tables[1].wait()
    route(blk, own, place, flag, seen, work, capacity=capacity, sizes=sizes)

    def compute(k, carry):
        gated = blk[0, k] == 0
        first, second, third = copies(k)
        first.wait()
        third.wait()
        pl.when(gated)(second.wait)
        g = gbuf[k].astype(jnp.float32)
        c = cbuf[k].astype(jnp.float32)
        s = jax.nn.sigmoid(g)
        first = jnp.where(gated, c * ubuf[k].astype(jnp.float32), c)
        act[k] = (first * jnp.where(gated, s * (1.0 + g * (1.0 - s)), g * s)).astype(act.dtype)
        return carry

    lax.fori_loop(0, listed, compute, 0, unroll=2)

    def end_rows(k, carry):
        pl.when(blk[1, k] // per == mine)(row_copy(k).wait)
        return carry

    lax.fori_loop(0, listed, end_rows, 0)
    for copy in state_copies:
        copy.wait()


def product_kernel(place, act, rows, *rest, shards, slots):
    others = rest[: shards - 1]
    send_a, send_b, part = rest[shards - 1 :]
    listed, _, size = act.shape
    per = others[0].shape[1] // size
    mine = lax.axis_index("tensor")

    def compute(k, carry):
        r = place[listed + k]
        cols = pl.ds(pl.multiple_of(lax.rem(r, per) * size, size), size)
        source = lax.rem(mine + shards - r // per, shards)
        lhs = rows[k]
        for j in range(1, shards):
            lhs = jnp.where(source == j, others[j - 1][:, cols], lhs)
        part[place[k]] = lax.dot_general(
            lhs, act[k], (((0,), (0,)), ((), ())), preferred_element_type=jnp.float32
        )
        return carry

    lax.fori_loop(0, listed, compute, 0, unroll=16)
    send_a[...] = part[:slots].astype(send_a.dtype)
    send_b[...] = part[2 * slots : 3 * slots].astype(send_b.dtype)


def add_kernel(part, got, total, send, *, start):
    total[...] = part[start : start + total.shape[0]] + got[...].astype(total.dtype)
    send[...] = total[...].astype(send.dtype)


def plane_kernel(place, sum_a, sum_b, other_a, other_b, *outs, listed, capacity):
    kept, sends = outs[0], outs[1:]
    slots = sum_a.shape[0]
    plane = lax.axis_index("dp") // COLUMNS

    def total(z, s):
        j = place[2 * listed + z * capacity + s]
        a = jnp.minimum(j, slots - 1)
        b = jnp.maximum(j - slots, 0)
        return jnp.where(
            j < slots,
            sum_a[a] + other_a[a].astype(jnp.float32),
            sum_b[b] + other_b[b].astype(jnp.float32),
        )

    if len(sends) == 1:
        sends = sends[0]

        def lay(j, carry):
            sends[j] = total(j // capacity, lax.rem(j, capacity)).astype(sends.dtype)
            return carry

        lax.fori_loop(0, sends.shape[0], lay, 0)
    else:
        for k, send in enumerate(sends):
            for s in range(capacity):
                send[s] = total(jnp.bitwise_xor(plane, k + 1), s).astype(send.dtype)
    for s in range(capacity):
        kept[s] = total(plane, s)


def update_kernel(place, kept, *rest, count):
    parts, rest = rest[:count], rest[count:]
    weights, moment1, moment2, *outs = rest
    outs, (bufs, sems) = outs[:3], outs[3:]
    held = place[place.shape[0] - 1]
    copies = []
    for s in range(kept.shape[0]):
        valid = s < held
        block_grad = kept[s]
        for part in parts:
            block_grad = block_grad + part[s].astype(jnp.float32)
        first_new = beta_first * moment1[s] + (1.0 - beta_first) * block_grad
        second_new = beta_second * moment2[s] + (1.0 - beta_second) * block_grad * block_grad
        weight_new = weights[s] - learn_rate * (first_new / bias_first) / (
            jnp.sqrt(second_new / bias_second) + epsilon
        )
        bufs[0, s] = jnp.where(valid, weight_new, weights[s])
        bufs[1, s] = jnp.where(valid, first_new, moment1[s])
        bufs[2, s] = jnp.where(valid, second_new, moment2[s])
        for i, out in enumerate(outs):
            copy = pltpu.make_async_copy(bufs.at[i, s], out.at[s], sems.at[i, s])
            copy.start()
            copies.append(copy)
    for copy in copies:
        copy.wait()


def local(features, gate_pre, up_pre, grad_hidden, blocks, owner, weights, moment1, moment2):
    size = weights.shape[-1]
    capacity = weights.shape[0]
    replicas = lax.axis_size("dp")
    shards = lax.axis_size("tensor")
    listed = owner.shape[0]
    tokens = features.shape[0]
    planes = replicas // COLUMNS
    sizes = bin_sizes(listed, replicas, capacity)
    bf16, f32 = jnp.bfloat16, jnp.float32
    block = size * size
    column = tokens * size
    in_vmem = lambda n, dtype: pltpu.VMEM((n, size, size), dtype)
    swap = lambda v, bit: lax.ppermute(v, "dp", [(i, i ^ bit) for i in range(replicas)])
    stay = lambda v: pltpu.with_memory_space_constraint(v, pltpu.HBM)
    grant = lambda nbytes: pltpu.CompilerParams(vmem_limit_bytes=nbytes * 5 // 4 + (4 << 20))

    others = [
        lax.ppermute(features, "tensor", [(i, (i + j) % shards) for i in range(shards)])
        for j in range(1, shards)
    ]
    act, rows, place, flag, *states = pl.pallas_call(
        functools.partial(act_kernel, capacity=capacity, sizes=sizes),
        out_shape=(
            pltpu.VMEM((listed, tokens, size), bf16),
            pltpu.VMEM((listed, tokens, size), bf16),
            pltpu.SMEM((2 * listed + planes * capacity + 1,), jnp.int32),
            pltpu.SMEM((1,), jnp.int32),
        )
        + (in_vmem(capacity, f32),) * 3,
        in_specs=[HBM] * 9,
        out_specs=(VMEM, VMEM, SMEM, SMEM, VMEM, VMEM, VMEM),
        scratch_shapes=[pltpu.VMEM((listed, tokens, size), bf16)] * 3
        + [
            pltpu.SMEM((3, listed), jnp.int32),
            pltpu.SMEM((listed,), jnp.int32),
            pltpu.SemaphoreType.DMA((4, listed)),
            pltpu.SemaphoreType.DMA((5,)),
            pltpu.SMEM((replicas,), jnp.int32),
            pltpu.SMEM((6 * COLUMNS,), jnp.int32),
        ],
        compiler_params=grant(5 * listed * column * 2 + 3 * capacity * block * 4),
        name="activations",
    )(*map(stay, (blocks.T, owner, features, gate_pre, up_pre, grad_hidden, weights, moment1, moment2)))
    direct = planes <= 4 and planes & (planes - 1) == 0

    def plane_sums(slots):
        send_a, send_b, part = pl.pallas_call(
            functools.partial(product_kernel, shards=shards, slots=slots),
            out_shape=(in_vmem(slots, bf16), in_vmem(slots, bf16), in_vmem(4 * slots, f32)),
            in_specs=[SMEM] + [VMEM] * (shards + 1),
            out_specs=(VMEM, VMEM, VMEM),
            compiler_params=grant(
                2 * listed * column * 2 + (shards - 1) * features.size * 2 + 20 * slots * block
            ),
            name="products",
        )(place, act, rows, *others)

        def add(got, start):
            return pl.pallas_call(
                functools.partial(add_kernel, start=start),
                out_shape=(in_vmem(slots, f32), in_vmem(slots, bf16)),
                in_specs=[VMEM, VMEM],
                out_specs=(VMEM, VMEM),
                compiler_params=grant(24 * slots * block),
                name="sums",
            )(part, got)

        sum_a, send_a = add(swap(send_a, 1), slots)
        sum_b, send_b = add(swap(send_b, 2), 3 * slots)
        other_a = swap(send_a, 2)
        other_b = swap(send_b, 1)
        return pl.pallas_call(
            functools.partial(plane_kernel, listed=listed, capacity=capacity),
            out_shape=(in_vmem(capacity, f32),)
            + ((in_vmem(capacity, bf16),) * (planes - 1) if direct else (in_vmem(planes * capacity, bf16),)),
            in_specs=[SMEM, VMEM, VMEM, VMEM, VMEM],
            out_specs=(VMEM,) * (planes if direct else 2),
            compiler_params=grant((12 * slots + (4 + 2 * planes) * capacity) * block),
            name="planes",
        )(place, sum_a, sum_b, other_a, other_b)

    kept, *sends = lax.switch(flag[0], [functools.partial(plane_sums, n) for n in sizes])
    if direct:
        parts = []
        for k, send in enumerate(sends):
            parts.append(swap(send, (k + 1) * COLUMNS))
    else:
        groups = [[z * COLUMNS + c for z in range(planes)] for c in range(COLUMNS)]
        incoming = lax.all_to_all(
            sends[0], "dp", split_axis=0, concat_axis=0, tiled=True, axis_index_groups=groups
        )
        away = jnp.arange(planes) != lax.axis_index("dp") // COLUMNS
        incoming = incoming.astype(f32).reshape(planes, capacity, size, size)
        parts = [jnp.sum(jnp.where(away[:, None, None, None], incoming, 0.0), axis=0)]
    return pl.pallas_call(
        functools.partial(update_kernel, count=len(parts)),
        out_shape=(jax.ShapeDtypeStruct(weights.shape, f32),) * 3,
        in_specs=[SMEM] + [VMEM] * (4 + len(parts)),
        out_specs=(HBM, HBM, HBM),
        scratch_shapes=[
            pltpu.VMEM((3,) + weights.shape, f32),
            pltpu.SemaphoreType.DMA((3, capacity)),
        ],
        compiler_params=grant((28 + 4 * len(parts)) * capacity * block),
        name="update",
    )(place, kept, *parts, *states)


def solution(mesh):
    cells = P(("dp", "tensor"), None, None)
    split = P("dp", "tensor")
    return jax.shard_map(
        local,
        mesh=mesh,
        in_specs=(split, split, split, split, P("tensor", None), P("tensor"), cells, cells, cells),
        out_specs=(cells, cells, cells),
        check_vma=False,
    )
```

```python
import functools
import jax
import jax.numpy as jnp
from jax import lax
from jax.experimental import pallas as pl
from jax.experimental.pallas import tpu as pltpu
from jax.sharding import PartitionSpec as P

beta_first = 0.9
beta_second = 0.999
learn_rate = 0.01
epsilon = 1e-08
bias_first = 1.0 - 0.9**10
bias_second = 1.0 - 0.999**10

HBM = pl.BlockSpec(memory_space=pltpu.HBM)
SMEM = pl.BlockSpec(memory_space=pltpu.SMEM)
VMEM = pl.BlockSpec(memory_space=pltpu.VMEM)

COLUMNS = 4


def bin_sizes(listed, replicas, capacity):
    crowd = min(listed, capacity * replicas // COLUMNS)
    level, most = -(-listed // COLUMNS), max(-(-listed // 3), -(-crowd // 2))
    return sorted({min(level, most), min(level + max(listed // 16, 1), most), most})


def route(blk, own, place, flag, depth, seen, work, *, capacity, sizes):
    listed = own.shape[0]
    replicas = seen.shape[0]
    me = lax.axis_index("dp")
    column = lax.rem(me, COLUMNS)
    my_bit = (lax.rem(column, 2), column // 2)
    COUNT, RANK, TAKE, AT_A, AT_B, LOAD = (i * COLUMNS for i in range(6))

    def clear_seen(o, carry):
        seen[o] = 0
        return carry

    lax.fori_loop(0, replicas, clear_seen, 0)
    for i in range(6 * COLUMNS):
        work[i] = 0

    def count(k, carry):
        q = lax.rem(own[k], COLUMNS)
        work[COUNT + q] = work[COUNT + q] + 1
        return carry

    lax.fori_loop(0, listed, count, 0)

    n = [work[COUNT + q] for q in range(COLUMNS)]

    def shares(size, a0):
        a2 = jnp.minimum(n[2], size - a0)
        a1 = n[1] - jnp.minimum(n[1], size - (n[0] - a0))
        a3 = jnp.minimum(n[3], size - a1)
        return a0, a1, a2, a3

    def search(size):
        low = jnp.maximum(n[0] - size, 0)
        high = jnp.minimum(n[0], size)

        def attempt(i, best):
            a = shares(size, low + i)
            ok = (low + i <= high) & (a[1] <= size) & (n[2] - a[2] + n[3] - a[3] <= size)
            return jnp.where(ok, low + i, best)

        return lax.fori_loop(0, size + 1, attempt, jnp.int32(-1))

    flag[0] = len(sizes) - 1
    work[LOAD + 1] = sizes[-1]
    work[LOAD] = search(sizes[-1])
    for i in reversed(range(len(sizes) - 1)):
        best = search(sizes[i])

        @pl.when(best >= 0)
        def _():
            flag[0] = i
            work[LOAD + 1] = sizes[i]
            work[LOAD] = best

    slots = work[LOAD + 1]
    a = shares(slots, work[LOAD])
    for q in range(COLUMNS):
        work[TAKE + q] = a[q]
    for q, (at_a, at_b) in enumerate(((0, 0), (0, n[0] - a[0]), (a[0], 0), (a[1], n[2] - a[2]))):
        work[AT_A + q] = at_a
        work[AT_B + q] = at_b

    def clear_place(j, carry):
        place[2 * listed + j] = 0
        return carry

    lax.fori_loop(0, replicas // COLUMNS * capacity, clear_place, 0)

    def assign(k, carry):
        o = own[k]
        q = lax.rem(o, COLUMNS)
        r = work[RANK + q]
        work[RANK + q] = r + 1
        take = work[TAKE + q]
        in_a = r < take
        slot = jnp.where(in_a, work[AT_A + q] + r, work[AT_B + q] + r - take)
        bit = jnp.where(in_a, lax.rem(q, 2), q // 2)
        mine = jnp.where(in_a, my_bit[0], my_bit[1])
        keep = (bit == mine).astype(jnp.int32)
        place[k] = jnp.where(in_a, 0, 2 * slots) + keep * slots + slot
        place[listed + k] = blk[1, k]
        s = seen[o]
        seen[o] = s + 1

        @pl.when(q == column)
        def _():
            place[2 * listed + o // COLUMNS * capacity + s] = jnp.where(in_a, 0, sizes[-1]) + slot

        return carry

    lax.fori_loop(0, listed, assign, 0)
    place[place.shape[0] - 1] = seen[me]
    busiest = jnp.int32(1)
    for z in range(replicas // COLUMNS):
        busiest = jnp.maximum(busiest, seen[z * COLUMNS + lax.rem(me, COLUMNS)])
    depth[0] = busiest - 1


def act_kernel(blk_hbm, own_hbm, features, gate, up, cot, *rest, capacity, sizes):
    states, rest = rest[:3], rest[3:]
    act, rows, place, flag, depth = rest[:5]
    held, (gbuf, ubuf, cbuf, blk, own, sems, state_sems, seen, work) = rest[5:8], rest[8:]
    listed, _, size = act.shape
    per = features.shape[1] // size
    mine = lax.axis_index("tensor")

    def row_copy(k):
        cols = pl.ds(pl.multiple_of(lax.rem(blk[1, k], per) * size, size), size)
        return pltpu.make_async_copy(features.at[:, cols], rows.at[k], sems.at[3, k])

    def copies(k):
        cols = pl.ds(pl.multiple_of(blk[2, k] * size, size), size)
        return [
            pltpu.make_async_copy(src.at[:, cols], buf.at[k], sems.at[i, k])
            for i, (src, buf) in enumerate(((gate, gbuf), (up, ubuf), (cot, cbuf)))
        ]

    def begin(k, carry):
        gated = blk[0, k] == 0
        first, second, third = copies(k)
        first.start()
        third.start()
        pl.when(gated)(second.start)
        return carry

    def begin_rows(k, carry):
        pl.when(blk[1, k] // per == mine)(row_copy(k).start)
        return carry

    tables = [
        pltpu.make_async_copy(blk_hbm, blk, state_sems.at[3]),
        pltpu.make_async_copy(own_hbm, own, state_sems.at[4]),
    ]
    for copy in tables:
        copy.start()
    tables[0].wait()
    lax.fori_loop(0, listed, begin, 0, unroll=2)
    lax.fori_loop(0, listed, begin_rows, 0, unroll=2)
    state_copies = [
        pltpu.make_async_copy(src, dst, state_sems.at[i])
        for i, (src, dst) in enumerate(zip(states, held))
    ]
    for copy in state_copies:
        copy.start()
    tables[1].wait()
    route(blk, own, place, flag, depth, seen, work, capacity=capacity, sizes=sizes)

    def compute(k, carry):
        gated = blk[0, k] == 0
        first, second, third = copies(k)
        first.wait()
        third.wait()
        pl.when(gated)(second.wait)
        g = gbuf[k].astype(jnp.float32)
        c = cbuf[k].astype(jnp.float32)
        s = jax.nn.sigmoid(g)
        first = jnp.where(gated, c * ubuf[k].astype(jnp.float32), c)
        act[k] = (first * jnp.where(gated, s * (1.0 + g * (1.0 - s)), g * s)).astype(act.dtype)
        return carry

    lax.fori_loop(0, listed, compute, 0, unroll=2)

    def end_rows(k, carry):
        pl.when(blk[1, k] // per == mine)(row_copy(k).wait)
        return carry

    lax.fori_loop(0, listed, end_rows, 0)
    for copy in state_copies:
        copy.wait()


def product_kernel(place, act, rows, *rest, shards, slots):
    others = rest[: shards - 1]
    send_a, send_b, part = rest[shards - 1 :]
    listed, _, size = act.shape
    per = others[0].shape[1] // size
    mine = lax.axis_index("tensor")

    def compute(k, carry):
        r = place[listed + k]
        cols = pl.ds(pl.multiple_of(lax.rem(r, per) * size, size), size)
        source = lax.rem(mine + shards - r // per, shards)
        lhs = rows[k]
        for j in range(1, shards):
            lhs = jnp.where(source == j, others[j - 1][:, cols], lhs)
        part[place[k]] = lax.dot_general(
            lhs, act[k], (((0,), (0,)), ((), ())), preferred_element_type=jnp.float32
        )
        return carry

    lax.fori_loop(0, listed, compute, 0, unroll=16)
    send_a[...] = part[:slots].astype(send_a.dtype)
    send_b[...] = part[2 * slots : 3 * slots].astype(send_b.dtype)


def add_kernel(part, got, total, send, *, start):
    total[...] = part[start : start + total.shape[0]] + got[...].astype(total.dtype)
    send[...] = total[...].astype(send.dtype)


def total_kernel(sum_a, sum_b, other_a, other_b, total):
    slots = sum_a.shape[0]
    most = total.shape[0] // 2
    total[:slots] = sum_a[...] + other_a[...].astype(total.dtype)
    total[most : most + slots] = sum_b[...] + other_b[...].astype(total.dtype)


def plane_kernel(place, total, *outs, listed, capacity):
    kept, sends = outs[0], outs[1:]
    plane = lax.axis_index("dp") // COLUMNS

    def cell(z, s):
        return total[place[2 * listed + z * capacity + s]]

    if len(sends) == 1:
        sends = sends[0]

        def lay(j, carry):
            sends[j] = cell(j // capacity, lax.rem(j, capacity)).astype(sends.dtype)
            return carry

        lax.fori_loop(0, sends.shape[0], lay, 0)
    else:
        for k, send in enumerate(sends):
            for s in range(send.shape[0]):
                send[s] = cell(jnp.bitwise_xor(plane, k + 1), s).astype(send.dtype)
    for s in range(kept.shape[0]):
        kept[s] = cell(plane, s)


def update_kernel(place, kept, *rest, count):
    parts, rest = rest[:count], rest[count:]
    weights, moment1, moment2, *outs = rest
    outs, (bufs, sems) = outs[:3], outs[3:]
    held = place[place.shape[0] - 1]
    copies = []
    for s in range(kept.shape[0], weights.shape[0]):
        for i, (state, out) in enumerate(zip((weights, moment1, moment2), outs)):
            copy = pltpu.make_async_copy(state.at[s], out.at[s], sems.at[i, s])
            copy.start()
            copies.append(copy)
    for s in range(kept.shape[0]):
        valid = s < held
        block_grad = kept[s]
        for part in parts:
            block_grad = block_grad + part[s].astype(jnp.float32)
        first_new = beta_first * moment1[s] + (1.0 - beta_first) * block_grad
        second_new = beta_second * moment2[s] + (1.0 - beta_second) * block_grad * block_grad
        weight_new = weights[s] - learn_rate * (first_new / bias_first) / (
            jnp.sqrt(second_new / bias_second) + epsilon
        )
        bufs[0, s] = jnp.where(valid, weight_new, weights[s])
        bufs[1, s] = jnp.where(valid, first_new, moment1[s])
        bufs[2, s] = jnp.where(valid, second_new, moment2[s])
        for i, out in enumerate(outs):
            copy = pltpu.make_async_copy(bufs.at[i, s], out.at[s], sems.at[i, s])
            copy.start()
            copies.append(copy)
    for copy in copies:
        copy.wait()


def local(features, gate_pre, up_pre, grad_hidden, blocks, owner, weights, moment1, moment2):
    size = weights.shape[-1]
    capacity = weights.shape[0]
    replicas = lax.axis_size("dp")
    shards = lax.axis_size("tensor")
    listed = owner.shape[0]
    tokens = features.shape[0]
    planes = replicas // COLUMNS
    sizes = bin_sizes(listed, replicas, capacity)
    bf16, f32 = jnp.bfloat16, jnp.float32
    block = size * size
    column = tokens * size
    in_vmem = lambda n, dtype: pltpu.VMEM((n, size, size), dtype)
    swap = lambda v, bit: lax.ppermute(v, "dp", [(i, i ^ bit) for i in range(replicas)])
    stay = lambda v: pltpu.with_memory_space_constraint(v, pltpu.HBM)
    grant = lambda nbytes: pltpu.CompilerParams(vmem_limit_bytes=nbytes * 5 // 4 + (4 << 20))

    others = [
        lax.ppermute(features, "tensor", [(i, (i + j) % shards) for i in range(shards)])
        for j in range(1, shards)
    ]
    act, rows, place, flag, depth, *states = pl.pallas_call(
        functools.partial(act_kernel, capacity=capacity, sizes=sizes),
        out_shape=(
            pltpu.VMEM((listed, tokens, size), bf16),
            pltpu.VMEM((listed, tokens, size), bf16),
            pltpu.SMEM((2 * listed + planes * capacity + 1,), jnp.int32),
            pltpu.SMEM((1,), jnp.int32),
            pltpu.SMEM((1,), jnp.int32),
        )
        + (in_vmem(capacity, f32),) * 3,
        in_specs=[HBM] * 9,
        out_specs=(VMEM, VMEM, SMEM, SMEM, SMEM, VMEM, VMEM, VMEM),
        scratch_shapes=[pltpu.VMEM((listed, tokens, size), bf16)] * 3
        + [
            pltpu.SMEM((3, listed), jnp.int32),
            pltpu.SMEM((listed,), jnp.int32),
            pltpu.SemaphoreType.DMA((4, listed)),
            pltpu.SemaphoreType.DMA((5,)),
            pltpu.SMEM((replicas,), jnp.int32),
            pltpu.SMEM((6 * COLUMNS,), jnp.int32),
        ],
        compiler_params=grant(5 * listed * column * 2 + 3 * capacity * block * 4),
        name="activations",
    )(*map(stay, (blocks.T, owner, features, gate_pre, up_pre, grad_hidden, weights, moment1, moment2)))
    direct = planes <= 4 and planes & (planes - 1) == 0

    def plane_sums(slots):
        send_a, send_b, part = pl.pallas_call(
            functools.partial(product_kernel, shards=shards, slots=slots),
            out_shape=(in_vmem(slots, bf16), in_vmem(slots, bf16), in_vmem(4 * slots, f32)),
            in_specs=[SMEM] + [VMEM] * (shards + 1),
            out_specs=(VMEM, VMEM, VMEM),
            compiler_params=grant(
                2 * listed * column * 2 + (shards - 1) * features.size * 2 + 20 * slots * block
            ),
            name="products",
        )(place, act, rows, *others)

        def add(got, start):
            return pl.pallas_call(
                functools.partial(add_kernel, start=start),
                out_shape=(in_vmem(slots, f32), in_vmem(slots, bf16)),
                in_specs=[VMEM, VMEM],
                out_specs=(VMEM, VMEM),
                compiler_params=grant(24 * slots * block),
                name="sums",
            )(part, got)

        sum_a, send_a = add(swap(send_a, 1), slots)
        sum_b, send_b = add(swap(send_b, 2), 3 * slots)
        other_a = swap(send_a, 2)
        other_b = swap(send_b, 1)
        return pl.pallas_call(
            total_kernel,
            out_shape=in_vmem(2 * sizes[-1], f32),
            in_specs=[VMEM] * 4,
            out_specs=VMEM,
            compiler_params=grant((12 * slots + 8 * sizes[-1]) * block),
            name="totals",
        )(sum_a, sum_b, other_a, other_b)

    total = lax.switch(flag[0], [functools.partial(plane_sums, n) for n in sizes])

    def finish(slots):
        outs = (slots,) * (planes - 1) if direct else (planes * capacity,)
        kept, *sends = pl.pallas_call(
            functools.partial(plane_kernel, listed=listed, capacity=capacity),
            out_shape=(in_vmem(slots, f32),) + tuple(in_vmem(n, bf16) for n in outs),
            in_specs=[SMEM, VMEM],
            out_specs=(VMEM,) * (1 + len(outs)),
            compiler_params=grant((8 * sizes[-1] + 4 * slots + 2 * sum(outs)) * block),
            name="planes",
        )(place, total)
        if direct:
            parts = []
            for k, send in enumerate(sends):
                parts.append(swap(send, (k + 1) * COLUMNS))
        else:
            groups = [[z * COLUMNS + c for z in range(planes)] for c in range(COLUMNS)]
            incoming = lax.all_to_all(
                sends[0], "dp", split_axis=0, concat_axis=0, tiled=True, axis_index_groups=groups
            )
            away = jnp.arange(planes) != lax.axis_index("dp") // COLUMNS
            incoming = incoming.astype(f32).reshape(planes, capacity, size, size)
            parts = [jnp.sum(jnp.where(away[:, None, None, None], incoming, 0.0), axis=0)]
        return pl.pallas_call(
            functools.partial(update_kernel, count=len(parts)),
            out_shape=(jax.ShapeDtypeStruct(weights.shape, f32),) * 3,
            in_specs=[SMEM] + [VMEM] * (4 + len(parts)),
            out_specs=(HBM, HBM, HBM),
            scratch_shapes=[
                pltpu.VMEM((3,) + weights.shape, f32),
                pltpu.SemaphoreType.DMA((3, capacity)),
            ],
            compiler_params=grant((28 + 4 * len(parts)) * capacity * block),
            name="update",
        )(place, kept, *parts, *states)

    if not direct:
        return finish(capacity)
    return lax.switch(depth[0], [functools.partial(finish, n) for n in range(1, capacity + 1)])


def solution(mesh):
    cells = P(("dp", "tensor"), None, None)
    split = P("dp", "tensor")
    return jax.shard_map(
        local,
        mesh=mesh,
        in_specs=(split, split, split, split, P("tensor", None), P("tensor"), cells, cells, cells),
        out_specs=(cells, cells, cells),
        check_vma=False,
    )
```

```python
import functools
import jax
import jax.numpy as jnp
from jax import lax
from jax.experimental import pallas as pl
from jax.experimental.pallas import tpu as pltpu
from jax.sharding import PartitionSpec as P

beta_first = 0.9
beta_second = 0.999
learn_rate = 0.01
epsilon = 1e-08
bias_first = 1.0 - 0.9**10
bias_second = 1.0 - 0.999**10

HBM = pl.BlockSpec(memory_space=pltpu.HBM)
SMEM = pl.BlockSpec(memory_space=pltpu.SMEM)
VMEM = pl.BlockSpec(memory_space=pltpu.VMEM)

COLUMNS = 4


def bin_sizes(listed, replicas, capacity):
    crowd = min(listed, capacity * replicas // COLUMNS)
    level, most = -(-listed // COLUMNS), max(-(-listed // 3), -(-crowd // 2))
    return sorted({min(level, most), min(level + max(listed // 16, 1), most), most})


def route(blk, own, place, flag, depth, seen, work, *, capacity, sizes):
    listed = own.shape[0]
    most = sizes[-1]
    cells = 4 * most + listed
    replicas = seen.shape[0]
    me = lax.axis_index("dp")
    column = lax.rem(me, COLUMNS)
    my_bit = (lax.rem(column, 2), column // 2)
    COUNT, RANK, TAKE, AT_A, AT_B, LOAD = (i * COLUMNS for i in range(6))

    def clear_seen(o, carry):
        seen[o] = 0
        return carry

    lax.fori_loop(0, replicas, clear_seen, 0, unroll=8)
    for i in range(6 * COLUMNS):
        work[i] = 0

    def count(k, carry):
        q = lax.rem(own[k], COLUMNS)
        work[COUNT + q] = work[COUNT + q] + 1
        return carry

    lax.fori_loop(0, listed, count, 0, unroll=4)

    n = [work[COUNT + q] for q in range(COLUMNS)]

    def shares(size, a0):
        a2 = jnp.minimum(n[2], size - a0)
        a1 = n[1] - jnp.minimum(n[1], size - (n[0] - a0))
        a3 = jnp.minimum(n[3], size - a1)
        return a0, a1, a2, a3

    def search(size):
        low = jnp.maximum(n[0] - size, 0)
        high = jnp.minimum(n[0], size)

        def attempt(i, best):
            a = shares(size, low + i)
            ok = (low + i <= high) & (a[1] <= size) & (n[2] - a[2] + n[3] - a[3] <= size)
            return jnp.where(ok, low + i, best)

        return lax.fori_loop(0, size + 1, attempt, jnp.int32(-1))

    def settle(i):
        best = search(sizes[i])
        flag[0] = i
        work[LOAD + 1] = sizes[i]
        work[LOAD] = best
        if i + 1 < len(sizes):
            pl.when(best < 0)(lambda: settle(i + 1))

    settle(0)
    a = shares(work[LOAD + 1], work[LOAD])
    for q in range(COLUMNS):
        work[TAKE + q] = a[q]
    for q, (at_a, at_b) in enumerate(((0, 0), (0, n[0] - a[0]), (a[0], 0), (a[1], n[2] - a[2]))):
        work[AT_A + q] = at_a
        work[AT_B + q] = at_b

    def clear_place(j, carry):
        place[cells + j] = 0
        return carry

    lax.fori_loop(0, replicas // COLUMNS * capacity, clear_place, 0, unroll=4)

    def clear_slots(j, carry):
        place[j] = 0
        return carry

    lax.fori_loop(0, 4 * most, clear_slots, 0, unroll=8)

    def assign(k, carry):
        o = own[k]
        q = lax.rem(o, COLUMNS)
        r = work[RANK + q]
        work[RANK + q] = r + 1
        take = work[TAKE + q]
        in_a = r < take
        slot = jnp.where(in_a, work[AT_A + q] + r, work[AT_B + q] + r - take)
        bit = jnp.where(in_a, lax.rem(q, 2), q // 2)
        mine = jnp.where(in_a, my_bit[0], my_bit[1])
        keep = (bit == mine).astype(jnp.int32)
        place[jnp.where(in_a, 0, 2 * most) + keep * most + slot] = k
        place[4 * most + k] = blk[1, k]
        s = seen[o]
        seen[o] = s + 1

        @pl.when(q == column)
        def _():
            place[cells + o // COLUMNS * capacity + s] = jnp.where(in_a, 0, most) + slot

        return carry

    lax.fori_loop(0, listed, assign, 0, unroll=4)
    place[place.shape[0] - 1] = seen[me]
    busiest = jnp.int32(1)
    for z in range(replicas // COLUMNS):
        busiest = jnp.maximum(busiest, seen[z * COLUMNS + lax.rem(me, COLUMNS)])
    depth[0] = busiest - 1


def act_kernel(blk_hbm, own_hbm, features, gate, up, cot, *rest, capacity, sizes):
    states, rest = rest[:3], rest[3:]
    act, rows, place, flag, depth = rest[:5]
    held, (gbuf, ubuf, cbuf, blk, own, sems, state_sems, seen, work) = rest[5:8], rest[8:]
    listed, _, size = act.shape
    per = features.shape[1] // size
    mine = lax.axis_index("tensor")

    def row_copy(k):
        cols = pl.ds(pl.multiple_of(lax.rem(blk[1, k], per) * size, size), size)
        return pltpu.make_async_copy(features.at[:, cols], rows.at[k], sems.at[3, k])

    def copies(k):
        cols = pl.ds(pl.multiple_of(blk[2, k] * size, size), size)
        return [
            pltpu.make_async_copy(src.at[:, cols], buf.at[k], sems.at[i, k])
            for i, (src, buf) in enumerate(((gate, gbuf), (up, ubuf), (cot, cbuf)))
        ]

    def begin(k, carry):
        gated = blk[0, k] == 0
        first, second, third = copies(k)
        first.start()
        third.start()
        pl.when(gated)(second.start)
        return carry

    def begin_rows(k, carry):
        pl.when(blk[1, k] // per == mine)(row_copy(k).start)
        return carry

    tables = [
        pltpu.make_async_copy(blk_hbm, blk, state_sems.at[3]),
        pltpu.make_async_copy(own_hbm, own, state_sems.at[4]),
    ]
    for copy in tables:
        copy.start()
    tables[0].wait()
    lax.fori_loop(0, listed, begin, 0, unroll=2)
    lax.fori_loop(0, listed, begin_rows, 0, unroll=2)
    state_copies = [
        pltpu.make_async_copy(src, dst, state_sems.at[i])
        for i, (src, dst) in enumerate(zip(states, held))
    ]
    for copy in state_copies:
        copy.start()
    tables[1].wait()
    route(blk, own, place, flag, depth, seen, work, capacity=capacity, sizes=sizes)

    def compute(k, carry):
        gated = blk[0, k] == 0
        first, second, third = copies(k)
        first.wait()
        third.wait()
        pl.when(gated)(second.wait)
        g = gbuf[k].astype(jnp.float32)
        c = cbuf[k].astype(jnp.float32)
        s = jax.nn.sigmoid(g)
        first = jnp.where(gated, c * ubuf[k].astype(jnp.float32), c)
        act[k] = (first * jnp.where(gated, s * (1.0 + g * (1.0 - s)), g * s)).astype(act.dtype)
        return carry

    lax.fori_loop(0, listed, compute, 0, unroll=2)

    def end_rows(k, carry):
        pl.when(blk[1, k] // per == mine)(row_copy(k).wait)
        return carry

    lax.fori_loop(0, listed, end_rows, 0)
    for copy in state_copies:
        copy.wait()


def product_kernel(place, act, rows, *rest, shards, most, bins):
    others, outs = rest[: shards - 1], rest[shards - 1 :]
    _, _, size = act.shape
    per = others[0].shape[1] // size
    mine = lax.axis_index("tensor")

    for out, at in zip(outs, bins):

        def compute(j, carry):
            k = place[at * most + j]
            r = place[4 * most + k]
            cols = pl.ds(pl.multiple_of(lax.rem(r, per) * size, size), size)
            source = lax.rem(mine + shards - r // per, shards)
            lhs = rows[k]
            for i in range(1, shards):
                lhs = jnp.where(source == i, others[i - 1][:, cols], lhs)
            out[j] = lax.dot_general(
                lhs, act[k], (((0,), (0,)), ((), ())), preferred_element_type=jnp.float32
            ).astype(out.dtype)
            return carry

        lax.fori_loop(0, out.shape[0], compute, 0, unroll=min(out.shape[0], 8))


def add_kernel(part, got, total, send):
    total[...] = part[...] + got[...].astype(total.dtype)
    send[...] = total[...].astype(send.dtype)


def total_kernel(sum_a, sum_b, other_a, other_b, total):
    slots = sum_a.shape[0]
    most = total.shape[0] // 2
    total[:slots] = sum_a[...] + other_a[...].astype(total.dtype)
    total[most : most + slots] = sum_b[...] + other_b[...].astype(total.dtype)


def plane_kernel(place, total, *outs, cells, capacity):
    kept, sends = outs[0], outs[1:]
    plane = lax.axis_index("dp") // COLUMNS

    def cell(z, s):
        return total[place[cells + z * capacity + s]]

    if len(sends) == 1:
        sends = sends[0]

        def lay(j, carry):
            sends[j] = cell(j // capacity, lax.rem(j, capacity)).astype(sends.dtype)
            return carry

        lax.fori_loop(0, sends.shape[0], lay, 0)
    else:
        for k, send in enumerate(sends):
            for s in range(send.shape[0]):
                send[s] = cell(jnp.bitwise_xor(plane, k + 1), s).astype(send.dtype)
    for s in range(kept.shape[0]):
        kept[s] = cell(plane, s)


def update_kernel(place, kept, *rest, count):
    parts, rest = rest[:count], rest[count:]
    weights, moment1, moment2, *outs = rest
    outs, (bufs, sems) = outs[:3], outs[3:]
    held = place[place.shape[0] - 1]
    copies = []
    for s in range(kept.shape[0], weights.shape[0]):
        for i, (state, out) in enumerate(zip((weights, moment1, moment2), outs)):
            copy = pltpu.make_async_copy(state.at[s], out.at[s], sems.at[i, s])
            copy.start()
            copies.append(copy)
    for s in range(kept.shape[0]):
        valid = s < held
        block_grad = kept[s]
        for part in parts:
            block_grad = block_grad + part[s].astype(jnp.float32)
        first_new = beta_first * moment1[s] + (1.0 - beta_first) * block_grad
        second_new = beta_second * moment2[s] + (1.0 - beta_second) * block_grad * block_grad
        weight_new = weights[s] - learn_rate * (first_new / bias_first) / (
            jnp.sqrt(second_new / bias_second) + epsilon
        )
        bufs[0, s] = jnp.where(valid, weight_new, weights[s])
        bufs[1, s] = jnp.where(valid, first_new, moment1[s])
        bufs[2, s] = jnp.where(valid, second_new, moment2[s])
        for i, out in enumerate(outs):
            copy = pltpu.make_async_copy(bufs.at[i, s], out.at[s], sems.at[i, s])
            copy.start()
            copies.append(copy)
    for copy in copies:
        copy.wait()


def local(features, gate_pre, up_pre, grad_hidden, blocks, owner, weights, moment1, moment2):
    size = weights.shape[-1]
    capacity = weights.shape[0]
    replicas = lax.axis_size("dp")
    shards = lax.axis_size("tensor")
    listed = owner.shape[0]
    tokens = features.shape[0]
    planes = replicas // COLUMNS
    sizes = bin_sizes(listed, replicas, capacity)
    bf16, f32 = jnp.bfloat16, jnp.float32
    block = size * size
    column = tokens * size
    in_vmem = lambda n, dtype: pltpu.VMEM((n, size, size), dtype)
    swap = lambda v, bit: lax.ppermute(v, "dp", [(i, i ^ bit) for i in range(replicas)])
    stay = lambda v: pltpu.with_memory_space_constraint(v, pltpu.HBM)
    grant = lambda nbytes: pltpu.CompilerParams(vmem_limit_bytes=nbytes * 5 // 4 + (4 << 20))

    others = [
        lax.ppermute(features, "tensor", [(i, (i + j) % shards) for i in range(shards)])
        for j in range(1, shards)
    ]
    act, rows, place, flag, depth, *states = pl.pallas_call(
        functools.partial(act_kernel, capacity=capacity, sizes=sizes),
        out_shape=(
            pltpu.VMEM((listed, tokens, size), bf16),
            pltpu.VMEM((listed, tokens, size), bf16),
            pltpu.SMEM((4 * sizes[-1] + listed + planes * capacity + 1,), jnp.int32),
            pltpu.SMEM((1,), jnp.int32),
            pltpu.SMEM((1,), jnp.int32),
        )
        + (in_vmem(capacity, f32),) * 3,
        in_specs=[HBM] * 9,
        out_specs=(VMEM, VMEM, SMEM, SMEM, SMEM, VMEM, VMEM, VMEM),
        scratch_shapes=[pltpu.VMEM((listed, tokens, size), bf16)] * 3
        + [
            pltpu.SMEM((3, listed), jnp.int32),
            pltpu.SMEM((listed,), jnp.int32),
            pltpu.SemaphoreType.DMA((4, listed)),
            pltpu.SemaphoreType.DMA((5,)),
            pltpu.SMEM((replicas,), jnp.int32),
            pltpu.SMEM((6 * COLUMNS,), jnp.int32),
        ],
        compiler_params=grant(5 * listed * column * 2 + 3 * capacity * block * 4),
        name="activations",
    )(*map(stay, (blocks.T, owner, features, gate_pre, up_pre, grad_hidden, weights, moment1, moment2)))
    direct = planes <= 4 and planes & (planes - 1) == 0

    def plane_sums(slots):
        def products(dtype, *bins):
            return pl.pallas_call(
                functools.partial(product_kernel, shards=shards, most=sizes[-1], bins=bins),
                out_shape=(in_vmem(slots, dtype),) * len(bins),
                in_specs=[SMEM] + [VMEM] * (shards + 1),
                out_specs=(VMEM,) * len(bins),
                compiler_params=grant(
                    2 * listed * column * 2 + (shards - 1) * features.size * 2 + 8 * slots * block
                ),
                name="products",
            )(place, act, rows, *others)

        def add(part, got):
            return pl.pallas_call(
                add_kernel,
                out_shape=(in_vmem(slots, f32), in_vmem(slots, bf16)),
                in_specs=[VMEM, VMEM],
                out_specs=(VMEM, VMEM),
                compiler_params=grant(12 * slots * block),
                name="sums",
            )(part, got)

        send_b, send_a = products(bf16, 2, 0)
        got_b = swap(send_b, 2)
        got_a = swap(send_a, 1)
        kept_b, kept_a = products(f32, 3, 1)
        sum_b, send_b = add(kept_b, got_b)
        sum_a, send_a = add(kept_a, got_a)
        other_b = swap(send_b, 1)
        other_a = swap(send_a, 2)
        return pl.pallas_call(
            total_kernel,
            out_shape=in_vmem(2 * sizes[-1], f32),
            in_specs=[VMEM] * 4,
            out_specs=VMEM,
            compiler_params=grant((12 * slots + 8 * sizes[-1]) * block),
            name="totals",
        )(sum_a, sum_b, other_a, other_b)

    total = lax.switch(flag[0], [functools.partial(plane_sums, n) for n in sizes])

    def finish(slots):
        outs = (slots,) * (planes - 1) if direct else (planes * capacity,)
        kept, *sends = pl.pallas_call(
            functools.partial(plane_kernel, cells=4 * sizes[-1] + listed, capacity=capacity),
            out_shape=(in_vmem(slots, f32),) + tuple(in_vmem(n, bf16) for n in outs),
            in_specs=[SMEM, VMEM],
            out_specs=(VMEM,) * (1 + len(outs)),
            compiler_params=grant((8 * sizes[-1] + 4 * slots + 2 * sum(outs)) * block),
            name="planes",
        )(place, total)
        if direct:
            parts = []
            for k, send in enumerate(sends):
                parts.append(swap(send, (k + 1) * COLUMNS))
        else:
            groups = [[z * COLUMNS + c for z in range(planes)] for c in range(COLUMNS)]
            incoming = lax.all_to_all(
                sends[0], "dp", split_axis=0, concat_axis=0, tiled=True, axis_index_groups=groups
            )
            away = jnp.arange(planes) != lax.axis_index("dp") // COLUMNS
            incoming = incoming.astype(f32).reshape(planes, capacity, size, size)
            parts = [jnp.sum(jnp.where(away[:, None, None, None], incoming, 0.0), axis=0)]
        return pl.pallas_call(
            functools.partial(update_kernel, count=len(parts)),
            out_shape=(jax.ShapeDtypeStruct(weights.shape, f32),) * 3,
            in_specs=[SMEM] + [VMEM] * (4 + len(parts)),
            out_specs=(HBM, HBM, HBM),
            scratch_shapes=[
                pltpu.VMEM((3,) + weights.shape, f32),
                pltpu.SemaphoreType.DMA((3, capacity)),
            ],
            compiler_params=grant((28 + 4 * len(parts)) * capacity * block),
            name="update",
        )(place, kept, *parts, *states)

    if not direct:
        return finish(capacity)
    return lax.switch(depth[0], [functools.partial(finish, n) for n in range(1, capacity + 1)])


def solution(mesh):
    cells = P(("dp", "tensor"), None, None)
    split = P("dp", "tensor")
    return jax.shard_map(
        local,
        mesh=mesh,
        in_specs=(split, split, split, split, P("tensor", None), P("tensor"), cells, cells, cells),
        out_specs=(cells, cells, cells),
        check_vma=False,
    )
```

```python
import functools
import jax
import jax.numpy as jnp
from jax import lax
from jax.experimental import pallas as pl
from jax.experimental.pallas import tpu as pltpu
from jax.sharding import PartitionSpec as P

beta_first = 0.9
beta_second = 0.999
learn_rate = 0.01
epsilon = 1e-08
bias_first = 1.0 - 0.9**10
bias_second = 1.0 - 0.999**10

HBM = pl.BlockSpec(memory_space=pltpu.HBM)
SMEM = pl.BlockSpec(memory_space=pltpu.SMEM)
VMEM = pl.BlockSpec(memory_space=pltpu.VMEM)

COLUMNS = 4


def bin_sizes(listed, replicas, capacity):
    crowd = min(listed, capacity * replicas // COLUMNS)
    level, most = -(-listed // COLUMNS), max(-(-listed // 3), -(-crowd // 2))
    step = max(listed // 16, 1)
    whole = [(n, n) for n in sorted({min(level, most), min(level + step, most), most})]
    small = (whole[0][0], whole[0][0] - step)
    return [small] * (0 < 2 * small[1] <= most) + whole


def route(blk, own, place, flag, depth, seen, work, *, capacity, sizes):
    listed = own.shape[0]
    most = sizes[-1][0]
    cells = 4 * most + listed
    starts = place.shape[0] - 5
    replicas = seen.shape[0]
    me = lax.axis_index("dp")
    column = lax.rem(me, COLUMNS)
    my_bit = (lax.rem(column, 2), column // 2)
    COUNT, RANK, TAKE, AT_A, AT_B, LOAD = (i * COLUMNS for i in range(6))

    def clear_seen(o, carry):
        seen[o] = 0
        return carry

    lax.fori_loop(0, replicas, clear_seen, 0, unroll=8)
    for i in range(6 * COLUMNS):
        work[i] = 0

    def count(k, carry):
        q = lax.rem(own[k], COLUMNS)
        work[COUNT + q] = work[COUNT + q] + 1
        return carry

    lax.fori_loop(0, listed, count, 0, unroll=4)

    n = [work[COUNT + q] for q in range(COLUMNS)]

    def shares(size, a0):
        a2 = jnp.minimum(n[2], size - a0)
        a1 = n[1] - jnp.minimum(n[1], size - (n[0] - a0))
        a3 = jnp.minimum(n[3], size - a1)
        return a0, a1, a2, a3

    def search(size, part):
        low = jnp.maximum(n[0] - size, 0)
        high = jnp.minimum(n[0], size)

        def attempt(i, best):
            a = shares(size, low + i)
            ok = (low + i <= high) & (a[1] <= size) & (n[2] - a[2] + n[3] - a[3] <= size)
            for q in range(COLUMNS):
                ok = ok & (jnp.maximum(a[q], n[q] - a[q]) <= part)
            return jnp.where(ok, low + i, best)

        return lax.fori_loop(0, size + 1, attempt, jnp.int32(-1))

    def settle(i):
        best = search(*sizes[i])
        flag[0] = i
        work[LOAD + 1] = sizes[i][0]
        work[LOAD] = best
        if i + 1 < len(sizes):
            pl.when(best < 0)(lambda: settle(i + 1))

    settle(0)
    a = shares(work[LOAD + 1], work[LOAD])
    for q in range(COLUMNS):
        work[TAKE + q] = a[q]
    for q, (at_a, at_b) in enumerate(((0, 0), (0, n[0] - a[0]), (a[0], 0), (a[1], n[2] - a[2]))):
        work[AT_A + q] = at_a
        work[AT_B + q] = at_b

    lo, hi = my_bit
    first_a = jnp.where(lo == 0, a[0], a[1])
    first_b = jnp.where(hi == 0, n[0] - a[0], n[2] - a[2])
    place[starts] = jnp.where(hi == 0, first_a, 0)
    place[starts + 1] = jnp.where(hi == 0, 0, first_a)
    place[starts + 2] = jnp.where(lo == 0, first_b, 0)
    place[starts + 3] = jnp.where(lo == 0, 0, first_b)

    def clear_place(j, carry):
        place[cells + j] = 0
        return carry

    lax.fori_loop(0, replicas // COLUMNS * capacity, clear_place, 0, unroll=4)

    def clear_slots(j, carry):
        place[j] = 0
        return carry

    lax.fori_loop(0, 4 * most, clear_slots, 0, unroll=8)

    def assign(k, carry):
        o = own[k]
        q = lax.rem(o, COLUMNS)
        r = work[RANK + q]
        work[RANK + q] = r + 1
        take = work[TAKE + q]
        in_a = r < take
        slot = jnp.where(in_a, work[AT_A + q] + r, work[AT_B + q] + r - take)
        bit = jnp.where(in_a, lax.rem(q, 2), q // 2)
        mine = jnp.where(in_a, my_bit[0], my_bit[1])
        keep = (bit == mine).astype(jnp.int32)
        place[jnp.where(in_a, 0, 2 * most) + keep * most + slot] = k
        place[4 * most + k] = blk[1, k]
        s = seen[o]
        seen[o] = s + 1

        @pl.when(q == column)
        def _():
            place[cells + o // COLUMNS * capacity + s] = jnp.where(in_a, 0, most) + slot

        return carry

    lax.fori_loop(0, listed, assign, 0, unroll=4)
    place[place.shape[0] - 1] = seen[me]
    busiest = jnp.int32(1)
    for z in range(replicas // COLUMNS):
        busiest = jnp.maximum(busiest, seen[z * COLUMNS + lax.rem(me, COLUMNS)])
    depth[0] = busiest - 1


def act_kernel(blk_hbm, own_hbm, features, gate, up, cot, *rest, capacity, sizes):
    states, rest = rest[:3], rest[3:]
    act, rows, place, flag, depth = rest[:5]
    held, (gbuf, ubuf, cbuf, blk, own, sems, state_sems, seen, work) = rest[5:8], rest[8:]
    listed, _, size = act.shape
    per = features.shape[1] // size
    mine = lax.axis_index("tensor")

    def row_copy(k):
        cols = pl.ds(pl.multiple_of(lax.rem(blk[1, k], per) * size, size), size)
        return pltpu.make_async_copy(features.at[:, cols], rows.at[k], sems.at[3, k])

    def copies(k):
        cols = pl.ds(pl.multiple_of(blk[2, k] * size, size), size)
        return [
            pltpu.make_async_copy(src.at[:, cols], buf.at[k], sems.at[i, k])
            for i, (src, buf) in enumerate(((gate, gbuf), (up, ubuf), (cot, cbuf)))
        ]

    def begin(k, carry):
        gated = blk[0, k] == 0
        first, second, third = copies(k)
        first.start()
        third.start()
        pl.when(gated)(second.start)
        return carry

    def begin_rows(k, carry):
        pl.when(blk[1, k] // per == mine)(row_copy(k).start)
        return carry

    tables = [
        pltpu.make_async_copy(blk_hbm, blk, state_sems.at[3]),
        pltpu.make_async_copy(own_hbm, own, state_sems.at[4]),
    ]
    for copy in tables:
        copy.start()
    tables[0].wait()
    lax.fori_loop(0, listed, begin, 0, unroll=2)
    lax.fori_loop(0, listed, begin_rows, 0, unroll=2)
    state_copies = [
        pltpu.make_async_copy(src, dst, state_sems.at[i])
        for i, (src, dst) in enumerate(zip(states, held))
    ]
    for copy in state_copies:
        copy.start()
    tables[1].wait()
    route(blk, own, place, flag, depth, seen, work, capacity=capacity, sizes=sizes)

    def compute(k, carry):
        gated = blk[0, k] == 0
        first, second, third = copies(k)
        first.wait()
        third.wait()
        pl.when(gated)(second.wait)
        g = gbuf[k].astype(jnp.float32)
        c = cbuf[k].astype(jnp.float32)
        s = jax.nn.sigmoid(g)
        first = jnp.where(gated, c * ubuf[k].astype(jnp.float32), c)
        act[k] = (first * jnp.where(gated, s * (1.0 + g * (1.0 - s)), g * s)).astype(act.dtype)
        return carry

    lax.fori_loop(0, listed, compute, 0, unroll=2)

    def end_rows(k, carry):
        pl.when(blk[1, k] // per == mine)(row_copy(k).wait)
        return carry

    lax.fori_loop(0, listed, end_rows, 0)
    for copy in state_copies:
        copy.wait()


def product_kernel(place, act, rows, *rest, shards, most, bins):
    others, outs = rest[: shards - 1], rest[shards - 1 :]
    _, _, size = act.shape
    per = others[0].shape[1] // size
    mine = lax.axis_index("tensor")

    for out, at in zip(outs, bins):

        def compute(j, carry):
            k = place[at * most + j]
            r = place[4 * most + k]
            cols = pl.ds(pl.multiple_of(lax.rem(r, per) * size, size), size)
            source = lax.rem(mine + shards - r // per, shards)
            lhs = rows[k]
            for i in range(1, shards):
                lhs = jnp.where(source == i, others[i - 1][:, cols], lhs)
            out[j] = lax.dot_general(
                lhs, act[k], (((0,), (0,)), ((), ())), preferred_element_type=jnp.float32
            ).astype(out.dtype)
            return carry

        lax.fori_loop(0, out.shape[0], compute, 0, unroll=min(out.shape[0], 8))


def add_kernel(place, part, got, total, send, *, bin):
    slots = total.shape[0]
    total[...] = part[...] + got[...].astype(total.dtype)
    if send.shape[0] == slots:
        send[...] = total[...].astype(send.dtype)
    else:
        start = place[place.shape[0] - 5 + 2 * bin]
        for j in range(send.shape[0]):
            send[j] = total[jnp.minimum(start + j, slots - 1)].astype(send.dtype)


def total_kernel(place, sum_a, sum_b, other_a, other_b, total):
    slots = sum_a.shape[0]
    for bin, (own, other) in enumerate(((sum_a, other_a), (sum_b, other_b))):
        at = bin * (total.shape[0] // 2)
        if other.shape[0] == slots:
            total[at : at + slots] = own[...] + other[...].astype(total.dtype)
        else:
            start = place[place.shape[0] - 4 + 2 * bin]
            for j in range(other.shape[0]):
                kept = own[jnp.minimum(start + j, slots - 1)]
                total[at + start + j] = kept + other[j].astype(total.dtype)


def plane_kernel(place, total, *outs, cells, capacity):
    kept, sends = outs[0], outs[1:]
    plane = lax.axis_index("dp") // COLUMNS

    def cell(z, s):
        return total[place[cells + z * capacity + s]]

    if len(sends) == 1:
        sends = sends[0]

        def lay(j, carry):
            sends[j] = cell(j // capacity, lax.rem(j, capacity)).astype(sends.dtype)
            return carry

        lax.fori_loop(0, sends.shape[0], lay, 0)
    else:
        for k, send in enumerate(sends):
            for s in range(send.shape[0]):
                send[s] = cell(jnp.bitwise_xor(plane, k + 1), s).astype(send.dtype)
    for s in range(kept.shape[0]):
        kept[s] = cell(plane, s)


def update_kernel(place, kept, *rest, count):
    parts, rest = rest[:count], rest[count:]
    weights, moment1, moment2, *outs = rest
    outs, (bufs, sems) = outs[:3], outs[3:]
    held = place[place.shape[0] - 1]
    copies = []
    for s in range(kept.shape[0], weights.shape[0]):
        for i, (state, out) in enumerate(zip((weights, moment1, moment2), outs)):
            copy = pltpu.make_async_copy(state.at[s], out.at[s], sems.at[i, s])
            copy.start()
            copies.append(copy)
    for s in range(kept.shape[0]):
        valid = s < held
        block_grad = kept[s]
        for part in parts:
            block_grad = block_grad + part[s].astype(jnp.float32)
        first_new = beta_first * moment1[s] + (1.0 - beta_first) * block_grad
        second_new = beta_second * moment2[s] + (1.0 - beta_second) * block_grad * block_grad
        weight_new = weights[s] - learn_rate * (first_new / bias_first) / (
            jnp.sqrt(second_new / bias_second) + epsilon
        )
        bufs[0, s] = jnp.where(valid, weight_new, weights[s])
        bufs[1, s] = jnp.where(valid, first_new, moment1[s])
        bufs[2, s] = jnp.where(valid, second_new, moment2[s])
        for i, out in enumerate(outs):
            copy = pltpu.make_async_copy(bufs.at[i, s], out.at[s], sems.at[i, s])
            copy.start()
            copies.append(copy)
    for copy in copies:
        copy.wait()


def local(features, gate_pre, up_pre, grad_hidden, blocks, owner, weights, moment1, moment2):
    size = weights.shape[-1]
    capacity = weights.shape[0]
    replicas = lax.axis_size("dp")
    shards = lax.axis_size("tensor")
    listed = owner.shape[0]
    tokens = features.shape[0]
    planes = replicas // COLUMNS
    sizes = bin_sizes(listed, replicas, capacity)
    bf16, f32 = jnp.bfloat16, jnp.float32
    block = size * size
    column = tokens * size
    in_vmem = lambda n, dtype: pltpu.VMEM((n, size, size), dtype)
    swap = lambda v, bit: lax.ppermute(v, "dp", [(i, i ^ bit) for i in range(replicas)])
    stay = lambda v: pltpu.with_memory_space_constraint(v, pltpu.HBM)
    grant = lambda nbytes: pltpu.CompilerParams(vmem_limit_bytes=nbytes * 5 // 4 + (4 << 20))

    others = [
        lax.ppermute(features, "tensor", [(i, (i + j) % shards) for i in range(shards)])
        for j in range(1, shards)
    ]
    act, rows, place, flag, depth, *states = pl.pallas_call(
        functools.partial(act_kernel, capacity=capacity, sizes=sizes),
        out_shape=(
            pltpu.VMEM((listed, tokens, size), bf16),
            pltpu.VMEM((listed, tokens, size), bf16),
            pltpu.SMEM((4 * sizes[-1][0] + listed + planes * capacity + 5,), jnp.int32),
            pltpu.SMEM((1,), jnp.int32),
            pltpu.SMEM((1,), jnp.int32),
        )
        + (in_vmem(capacity, f32),) * 3,
        in_specs=[HBM] * 9,
        out_specs=(VMEM, VMEM, SMEM, SMEM, SMEM, VMEM, VMEM, VMEM),
        scratch_shapes=[pltpu.VMEM((listed, tokens, size), bf16)] * 3
        + [
            pltpu.SMEM((3, listed), jnp.int32),
            pltpu.SMEM((listed,), jnp.int32),
            pltpu.SemaphoreType.DMA((4, listed)),
            pltpu.SemaphoreType.DMA((5,)),
            pltpu.SMEM((replicas,), jnp.int32),
            pltpu.SMEM((6 * COLUMNS,), jnp.int32),
        ],
        compiler_params=grant(5 * listed * column * 2 + 3 * capacity * block * 4),
        name="activations",
    )(*map(stay, (blocks.T, owner, features, gate_pre, up_pre, grad_hidden, weights, moment1, moment2)))
    direct = planes <= 4 and planes & (planes - 1) == 0

    def plane_sums(slots, some):
        def products(dtype, *bins):
            return pl.pallas_call(
                functools.partial(product_kernel, shards=shards, most=sizes[-1][0], bins=bins),
                out_shape=(in_vmem(slots, dtype),) * len(bins),
                in_specs=[SMEM] + [VMEM] * (shards + 1),
                out_specs=(VMEM,) * len(bins),
                compiler_params=grant(
                    2 * listed * column * 2 + (shards - 1) * features.size * 2 + 8 * slots * block
                ),
                name="products",
            )(place, act, rows, *others)

        def add(part, got, bin):
            return pl.pallas_call(
                functools.partial(add_kernel, bin=bin),
                out_shape=(in_vmem(slots, f32), in_vmem(some, bf16)),
                in_specs=[SMEM, VMEM, VMEM],
                out_specs=(VMEM, VMEM),
                compiler_params=grant(12 * slots * block),
                name="sums",
            )(place, part, got)

        send_b, send_a = products(bf16, 2, 0)
        got_b = swap(send_b, 2)
        got_a = swap(send_a, 1)
        kept_b, kept_a = products(f32, 3, 1)
        sum_b, send_b = add(kept_b, got_b, 1)
        sum_a, send_a = add(kept_a, got_a, 0)
        other_b = swap(send_b, 1)
        other_a = swap(send_a, 2)
        return pl.pallas_call(
            total_kernel,
            out_shape=in_vmem(2 * sizes[-1][0], f32),
            in_specs=[SMEM] + [VMEM] * 4,
            out_specs=VMEM,
            compiler_params=grant((12 * slots + 8 * sizes[-1][0]) * block),
            name="totals",
        )(place, sum_a, sum_b, other_a, other_b)

    total = lax.switch(flag[0], [functools.partial(plane_sums, *n) for n in sizes])

    def finish(slots):
        outs = (slots,) * (planes - 1) if direct else (planes * capacity,)
        kept, *sends = pl.pallas_call(
            functools.partial(plane_kernel, cells=4 * sizes[-1][0] + listed, capacity=capacity),
            out_shape=(in_vmem(slots, f32),) + tuple(in_vmem(n, bf16) for n in outs),
            in_specs=[SMEM, VMEM],
            out_specs=(VMEM,) * (1 + len(outs)),
            compiler_params=grant((8 * sizes[-1][0] + 4 * slots + 2 * sum(outs)) * block),
            name="planes",
        )(place, total)
        if direct:
            parts = []
            for k, send in enumerate(sends):
                parts.append(swap(send, (k + 1) * COLUMNS))
        else:
            groups = [[z * COLUMNS + c for z in range(planes)] for c in range(COLUMNS)]
            incoming = lax.all_to_all(
                sends[0], "dp", split_axis=0, concat_axis=0, tiled=True, axis_index_groups=groups
            )
            away = jnp.arange(planes) != lax.axis_index("dp") // COLUMNS
            incoming = incoming.astype(f32).reshape(planes, capacity, size, size)
            parts = [jnp.sum(jnp.where(away[:, None, None, None], incoming, 0.0), axis=0)]
        return pl.pallas_call(
            functools.partial(update_kernel, count=len(parts)),
            out_shape=(jax.ShapeDtypeStruct(weights.shape, f32),) * 3,
            in_specs=[SMEM] + [VMEM] * (4 + len(parts)),
            out_specs=(HBM, HBM, HBM),
            scratch_shapes=[
                pltpu.VMEM((3,) + weights.shape, f32),
                pltpu.SemaphoreType.DMA((3, capacity)),
            ],
            compiler_params=grant((28 + 4 * len(parts)) * capacity * block),
            name="update",
        )(place, kept, *parts, *states)

    if not direct:
        return finish(capacity)
    return lax.switch(depth[0], [functools.partial(finish, n) for n in range(1, capacity + 1)])


def solution(mesh):
    cells = P(("dp", "tensor"), None, None)
    split = P("dp", "tensor")
    return jax.shard_map(
        local,
        mesh=mesh,
        in_specs=(split, split, split, split, P("tensor", None), P("tensor"), cells, cells, cells),
        out_specs=(cells, cells, cells),
        check_vma=False,
    )
```
